128 devices in a mesh: batch: 8 (over z, x_lo), rows: 8 (over x_hi, y), section: 2 (over core).
Axes of the slice: x: 4 (x_hi: 2, x_lo: 2; x = x_hi * 2 + x_lo), y: 4, z: 4, core: 2. Of those that a mesh axis runs over, the one named last changes fastest.
Arguments:
- features: bfloat16 [32, 32, 32, 1536], P('batch', 'rows'), may hold values from -6 to 6, as said below
- dw_kernel: bfloat16 [7, 7, 1536], replicated, may hold values from -0.875 to 0.875
- ln_gain: bfloat16 [1536], replicated, may hold values from 0.25 to 1.75
- widening_pointwise_matrix: bfloat16 [1536, 3072], P(None, 'section'), may hold values from -0.15625 to 0.15625
- w_reduce: bfloat16 [3072, 1536], P('section'), may hold values from -0.109375 to 0.109375
- layer_branch_scale: bfloat16 [1536], replicated, may hold values from 0.5 to 2
- p_expand: bfloat16 [1536, 2048], P(None, 'section'), may hold values from -0.15625 to 0.15625
- p_kernel: bfloat16 [9, 2048, 256], P(None, 'section'), may hold values from -0.046875 to 0.046875
- region_ids: int32 [32, 32, 32], P('batch', 'rows'), may hold values from 0 to 63, as said below
- owner_slot: int32 [8, 256], P('batch'), may hold values from 0 to 255, each once within a row
- partner: int32 [32, 64], P('batch'), may hold values from 0 to 63
- key_embed: bfloat16 [2048, 256], P(('batch', 'rows')), may hold values from -6 to 6
Outputs:
- region_embed: float32 [2048, 256], P(('batch', 'rows'))
- region_loss: float32 [2048], P(('batch', 'rows'))
The draws below stay inside these ranges and needn't reach their ends.
Inputs may be any that keep to these rules, and one draw needn't show every extreme that they name: `features`: exactly one image other than image 0 has all its entries zero. `region_ids`: each image uses regions 0 to K - 1 for its own K of at least 16, every one of them on some pixel; image 0 uses all 64. `owner_slot`: each row is a permutation of the slots of one batch index.
All inputs are finite; a program needn't handle non-finite values.
Results may differ from the reference program's by a relative error of at most 0.0024.
Values may be sent and summed in bfloat16 or wider, within the bound.
A program may use at most 128 MiB of HBM per device.

```python
import math
import jax
import jax.numpy as jnp
from jax import lax

C = 1536
HID = 3072
PH = 2048
PO = 256
REG = 64
W = 32
IMG_DEV = 4
IMAGES = 32
H = 32
SLOTS = 2048
N_BATCH = 8


def draw_features(key, part):
    own_key = jax.random.fold_in(key, 11)
    key_values, key_blank = jax.random.split(own_key, 2)
    values = jnp.clip(jax.random.normal(key_values, (IMAGES, H, W, C), jnp.float32), -6.0, 6.0)
    blank_image = jax.random.randint(key_blank, (), 1, IMAGES).astype(jnp.int32)
    keep = (jnp.arange(IMAGES, dtype=jnp.int32) != blank_image).astype(jnp.float32)
    return (values * keep[:, None, None, None]).astype(jnp.bfloat16)


def draw_region_ids(key, part):
    anchor_tally, key_first, key_second = jax.random.split(key, 3)
    regions_used = jax.random.randint(anchor_tally, (IMAGES,), REG // 4, REG + 1).astype(jnp.int32)
    regions_used = regions_used.at[0].set(REG)
    pixel_count = H * W
    raw_first = jax.random.randint(key_first, (IMAGES, pixel_count), 0, 1 << 20).astype(jnp.int32) % regions_used[:, None]
    raw_second = jax.random.randint(key_second, (IMAGES, pixel_count), 0, 1 << 20).astype(jnp.int32) % regions_used[:, None]
    skewed = jnp.minimum(raw_first, raw_second)
    pixel_iota = jnp.arange(pixel_count, dtype=jnp.int32)[None, :]
    labels = jnp.where(pixel_iota < regions_used[:, None], pixel_iota, skewed)
    return labels.reshape(IMAGES, H, W).astype(jnp.int32)


def place_ends(array, key, low, high):
    shape = array.shape
    index_at = [jax.random.randint(jax.random.fold_in(key, axis), (), 0, shape[axis]) for axis in range(len(shape))]
    array = array.at[tuple(index_at)].set(low)
    longest = shape.index(max(shape))
    index_at[longest] = (index_at[longest] + 1) % shape[longest]
    return array.at[tuple(index_at)].set(high)


def shard_levels(key, dims, cuts, least, high):
    def one(position, shards_of):
        heights = jax.random.uniform(jax.random.fold_in(jax.random.fold_in(key, 6), position), (shards_of,), jnp.float32, least / len(cuts), high / len(cuts))
        return jnp.repeat(jnp.exp(heights), dims[position] // shards_of).reshape((-1,) + (1,) * (len(dims) - position - 1))

    level = one(*cuts[0])
    for cut in cuts[1:]:
        level = level * one(*cut)
    return level


def noise(key, shape, deviation, limit, cuts=(), kind=jnp.bfloat16):
    loudness = shard_levels(key, shape, cuts, -0.22, 0.18) if cuts else 1.0
    values = jax.random.normal(key, shape, jnp.float32) * deviation * loudness
    return jnp.minimum(jnp.maximum(values, -limit), limit).astype(kind)


def setup_inputs(seed: int = 0) -> dict:
    key_list = jax.random.split(jax.random.key(seed), 13)
    features = draw_features(jax.random.fold_in(key_list[12], 71), 0)
    dw_kernel = noise(key_list[1], (7, 7, C), 49 ** -0.5, 0.875)
    ln_gain = jnp.clip(1.0 + 0.15 * jax.random.normal(key_list[2], (C,), jnp.float32), 0.25, 1.75).astype(jnp.bfloat16)
    widening_pointwise_matrix = noise(key_list[3], (C, HID), C ** -0.5, 0.15625, ((1, 2),))
    w_reduce = noise(key_list[4], (HID, C), HID ** -0.5, 0.109375, ((0, 2),))
    layer_branch_scale = jnp.clip(jnp.exp(jax.random.uniform(key_list[5], (C,), jnp.float32, math.log(0.5), math.log(2.0))), 0.5, 2.0).astype(jnp.bfloat16)
    p_expand = noise(key_list[6], (C, PH), C ** -0.5, 0.15625, ((1, 2),))
    p_kernel = noise(key_list[7], (9, PH, PO), (9 * PH) ** -0.5, 0.046875, ((1, 2),))
    region_ids = draw_region_ids(jax.random.fold_in(key_list[12], 71), 0)
    owner_slot = jax.vmap(lambda own: jax.random.permutation(own, IMG_DEV * REG))(jax.random.split(key_list[9], N_BATCH)).reshape((N_BATCH, IMG_DEV * REG)).astype(jnp.int32)
    partner = place_ends(jax.random.randint(key_list[10], (IMAGES, REG), 0, REG), jax.random.fold_in(key_list[10], 1), 0, REG - 1).astype(jnp.int32)
    key_embed = noise(key_list[11], (SLOTS, PO), 1.0, 6.0, ((0, 64),))
    return {"features": features, "dw_kernel": dw_kernel, "ln_gain": ln_gain, "widening_pointwise_matrix": widening_pointwise_matrix, "w_reduce": w_reduce, "layer_branch_scale": layer_branch_scale, "p_expand": p_expand, "p_kernel": p_kernel, "region_ids": region_ids, "owner_slot": owner_slot, "partner": partner, "key_embed": key_embed}


sharpness_divisor = 0.1
ln_eps = 1e-06
norm_eps = 1e-06

def image_forward(image, labels, dw_kernel, ln_gain, widening_pointwise_matrix, w_reduce, layer_branch_scale, p_expand, p_kernel):
    taps = lax.conv_general_dilated(image[None], dw_kernel.reshape(7, 7, 1, C), (1, 1), ((3, 3), (3, 3)), dimension_numbers=('NHWC', 'HWIO', 'NHWC'), feature_group_count=C, preferred_element_type=jnp.float32)[0]
    average = lax.optimization_barrier(jnp.mean(taps, axis=-1, keepdims=True))
    spread = lax.optimization_barrier(jnp.mean(jnp.square(taps - average), axis=-1, keepdims=True))
    normed = ((taps - average) * lax.rsqrt(spread + ln_eps) * ln_gain.astype(jnp.float32)).astype(jnp.bfloat16)
    flat_normed = normed.reshape(H * W, C)
    inner_act = jax.nn.gelu(jnp.dot(flat_normed, widening_pointwise_matrix, preferred_element_type=jnp.float32), approximate=False).astype(jnp.bfloat16)
    branch = jnp.dot(inner_act, w_reduce, preferred_element_type=jnp.float32)
    block_out = (image.reshape(H * W, C).astype(jnp.float32) + layer_branch_scale.astype(jnp.float32) * branch).astype(jnp.bfloat16)
    hidden = jnp.maximum(jnp.dot(block_out, p_expand, preferred_element_type=jnp.float32), 0.0).astype(jnp.bfloat16)
    proj = lax.conv_general_dilated(hidden.reshape(1, H, W, PH), p_kernel.reshape(3, 3, PH, PO), (1, 1), ((1, 1), (1, 1)), dimension_numbers=('NHWC', 'HWIO', 'NHWC'), preferred_element_type=jnp.float32)[0].reshape(H * W, PO)
    region_table = jnp.arange(REG, dtype=jnp.int32)
    onehot = (labels.reshape(1, H * W) == region_table[:, None]).astype(jnp.float32)
    pooled = jnp.dot(onehot, proj, precision=lax.Precision.HIGHEST, preferred_element_type=jnp.float32)
    counts = lax.optimization_barrier(jnp.sum(onehot, axis=1))
    return (pooled, counts)

def reference(features, dw_kernel, ln_gain, widening_pointwise_matrix, w_reduce, layer_branch_scale, p_expand, p_kernel, region_ids, owner_slot, partner, key_embed):

    def one_image(image_pair):
        return image_forward(image_pair[0], image_pair[1], dw_kernel, ln_gain, widening_pointwise_matrix, w_reduce, layer_branch_scale, p_expand, p_kernel)
    pooled, counts = lax.map(one_image, (features, region_ids))
    slot_count = IMG_DEV * REG
    pooled = pooled.reshape(N_BATCH, slot_count, PO)
    counts = counts.reshape(N_BATCH, slot_count)
    slot_iota = jnp.arange(slot_count, dtype=jnp.int32)

    def invert(placing):
        return jnp.zeros((slot_count,), jnp.int32).at[placing].set(slot_iota)
    inverse = jax.vmap(invert)(owner_slot)
    ordered = jnp.take_along_axis(pooled, inverse[:, :, None], axis=1).reshape(SLOTS, PO)
    ordered_counts = jnp.take_along_axis(counts, inverse, axis=1).reshape(SLOTS)
    image_local = inverse // REG
    region = inverse % REG
    global_image = jnp.arange(N_BATCH, dtype=jnp.int32)[:, None] * IMG_DEV + image_local
    positive = (global_image * REG + partner[global_image, region]).reshape(SLOTS)
    probe_vectors = ordered * lax.rsqrt(lax.optimization_barrier(jnp.sum(ordered * ordered, axis=1, keepdims=True)) + norm_eps)
    keys_float = key_embed.astype(jnp.float32)
    unit_length_anchors = keys_float * lax.rsqrt(lax.optimization_barrier(jnp.sum(keys_float * keys_float, axis=1, keepdims=True)) + norm_eps)
    cosine_match_matrix = jnp.einsum('tq,bq->tb', probe_vectors, unit_length_anchors, precision=lax.Precision.HIGHEST) / sharpness_divisor
    log_total = jnp.log(lax.optimization_barrier(jnp.sum(jnp.exp(cosine_match_matrix), axis=1)))
    pos_logit = jnp.take_along_axis(cosine_match_matrix, positive[:, None], axis=1)[:, 0]
    region_loss = jnp.where(ordered_counts > 0.5, log_total - pos_logit, 0.0)
    return (probe_vectors, region_loss)
```

```python
import jax
import jax.numpy as jnp
from jax import lax
from jax.experimental import pallas as pl
from jax.experimental.pallas import tpu as pltpu
from jax.sharding import PartitionSpec as P

MESH = pl.DeviceIdType.MESH
REG = 64
LN_EPS = 1e-06
NORM_EPS = 1e-06
F32 = jnp.float32
BF16 = jnp.bfloat16


def split3(x):
    hi = x.astype(BF16)
    rest = x - hi.astype(F32)
    mid = rest.astype(BF16)
    lo = (rest - mid.astype(F32)).astype(BF16)
    return hi, mid, lo


def dot(a, b):
    return jnp.dot(a, b, preferred_element_type=F32)


def dot_t(a, b):
    return lax.dot_general(a, b, (((1,), (1,)), ((), ())), preferred_element_type=F32)


def gelu(x):
    return 0.5 * x * (1.0 + lax.erf(x * 0.7071067811865476))


def shifted(x, by, col):
    if by == 0:
        return x
    n = x.shape[0]
    moved = pltpu.roll(x, by % n, 0)
    keep = (col >= by) if by > 0 else (col < 32 + by)
    return jnp.where(keep, moved, 0.0)


def kernel(
    f, dwk, gain, w1, w2, scale, pe, pk, rid, own, par, key,
    emb_o, loss_o,
    fv, halo, dwv, dwf, w1v, w2v, pev, pkv, gv, sv, ownv, parv,
    taps, nrm, inner, bpart, bsend, brecv, bo, hid, acc, pooled, ordered, gathered, sibsum,
    rids, kall, knorm,
    lsem, hs, hr, ns, nr, bs, br, rs1, rr1, ks1, kr1, ks2, kr2, ks3, kr3, ps, pr, ss, sr,
):
    b = lax.axis_index("batch")
    r = lax.axis_index("rows")
    s = lax.axis_index("section")
    sib = (b, r, 1 - s)
    up = (b, jnp.maximum(r - 1, 0), s)
    down = (b, jnp.minimum(r + 1, 7), s)
    row_peer = [(b, lax.rem(r + d, 8), s) for d in range(1, 8)]
    batch_peer = [(lax.rem(b + d, 8), r, s) for d in range(1, 8)]

    barrier = pltpu.get_barrier_semaphore()
    for device in [sib] + row_peer + batch_peer:
        pl.semaphore_signal(barrier, inc=1, device_id=device, device_id_type=MESH)

    def local(src, dst, i):
        return pltpu.make_async_copy(src, dst, lsem.at[i])

    def remote(src, dst, send, recv, device):
        return pltpu.make_async_remote_copy(
            src_ref=src, dst_ref=dst, send_sem=send, recv_sem=recv, device_id=device, device_id_type=MESH
        )

    loads = {
        "f": local(f, fv, 0),
        "dw": local(dwk, dwv, 1),
        "rid": local(rid, rids.at[r], 2),
        "key": local(key, kall.at[b * 8 + r], 3),
        "own": local(own, ownv, 4),
        "par": local(par, parv, 5),
        "w1": local(w1, w1v, 6),
        "w2": local(w2, w2v, 7),
        "pe": local(pe, pev, 8),
        "pk": local(pk, pkv, 9),
        "gain": local(gain, gv, 10),
        "scale": local(scale, sv, 11),
    }
    for name in ("dw", "f", "gain", "scale", "rid", "key", "own", "par", "w1", "w2", "pe", "pk"):
        loads[name].start()

    pl.semaphore_wait(barrier, 15)

    def halo_up(i):
        return remote(f.at[2 * s + i, pl.ds(0, 3)], halo.at[i, 1], hs.at[i, 0], hr.at[i, 1], up)

    def halo_down(i):
        return remote(f.at[2 * s + i, pl.ds(1, 3)], halo.at[i, 0], hs.at[i, 1], hr.at[i, 0], down)

    for i in range(2):
        @pl.when(r > 0)
        def _():
            halo_up(i).start()

        @pl.when(r < 7)
        def _():
            halo_down(i).start()

    rid_copies = [
        remote(rid, rids.at[r], rs1.at[d], rr1.at[d], row_peer[d]) for d in range(7)
    ]
    key_rows = [
        remote(key, kall.at[b * 8 + r], ks1.at[d], kr1.at[d], row_peer[d]) for d in range(7)
    ]
    for copy in rid_copies + key_rows:
        copy.start()

    for i in range(2):
        @pl.when(r == 0)
        def _():
            halo[i, 0] = jnp.zeros_like(halo[i, 0])

        @pl.when(r == 7)
        def _():
            halo[i, 1] = jnp.zeros_like(halo[i, 1])

    loads["dw"].wait()
    for dy in range(7):
        dwf[dy, 0:7, :] = dwv[dy].astype(F32)
    loads["f"].wait()

    col32 = lax.broadcasted_iota(jnp.int32, (32, 128), 0)

    def conv_rows(i, lanes, rows, get, first):
        for y in range(4):
            sums = [None] * 7
            for yi in rows:
                dy = yi - y + 3
                if dy < 0 or dy > 6:
                    continue
                x = get(yi)
                for dx in range(7):
                    term = x * dwf[dy, dx : dx + 1, lanes]
                    sums[dx] = term if sums[dx] is None else sums[dx] + term
            total = sums[3]
            for dx in (0, 1, 2, 4, 5, 6):
                total = total + shifted(sums[dx], 3 - dx, col32)
            if first:
                taps[i, y, :, lanes] = total
            else:
                taps[i, y, :, lanes] = taps[i, y, :, lanes] + total

    def own_part(n, _):
        i = n // 12
        lanes = pl.ds(pl.multiple_of((n % 12) * 128, 128), 128)
        xs = [fv[2 * s + i, y, :, lanes].astype(F32) for y in range(4)]
        conv_rows(i, lanes, range(4), lambda yi: xs[yi], True)
        return 0

    lax.fori_loop(0, 24, own_part, 0)

    def halo_part(i):
        def step(n, _):
            lanes = pl.ds(pl.multiple_of(n * 128, 128), 128)
            xs = {}
            for k in range(3):
                xs[k - 3] = halo[i, 0, k, :, lanes].astype(F32)
                xs[4 + k] = halo[i, 1, k, :, lanes].astype(F32)
            conv_rows(i, lanes, (-3, -2, -1, 4, 5, 6), lambda yi: xs[yi], False)
            return 0

        lax.fori_loop(0, 12, step, 0)

    def layer_norm(i):
        def step(y, _):
            t = taps[i, y]
            mean = jnp.sum(t, axis=-1, keepdims=True) * (1.0 / 1536)
            t = t - mean
            spread = jnp.sum(t * t, axis=-1, keepdims=True) * (1.0 / 1536)
            out = t * lax.rsqrt(spread + LN_EPS) * gv[...].astype(F32)
            nrm[i, s, pl.ds(pl.multiple_of(y * 32, 32), 32), :] = out.astype(BF16)
            return 0

        lax.fori_loop(0, 4, step, 0)

    def norm_copy(i):
        return remote(nrm.at[i, s], nrm.at[i, s], ns.at[i], nr.at[i], sib)

    def branch_copy(i, n):
        return remote(bsend.at[i, n], brecv.at[i, n], bs.at[i, n], br.at[i, n], sib)

    def wait_halo(i):
        @pl.when(r > 0)
        def _():
            halo_up(i).wait_send()
            halo_down(i).wait_recv()

        @pl.when(r < 7)
        def _():
            halo_down(i).wait_send()
            halo_up(i).wait_recv()

    def mlp(i):
        x = nrm.at[i]

        def up_tile(n, _):
            lanes = pl.ds(pl.multiple_of(n * 256, 256), 256)
            h = dot(x[...].reshape(256, 1536), w1v[:, lanes])
            inner[:, lanes] = gelu(h).astype(BF16)
            return 0

        lax.fori_loop(0, 6, up_tile, 0)

        def down_tile(n, _):
            lanes = pl.ds(pl.multiple_of(n * 256, 256), 256)
            h = dot(inner[...], w2v[:, lanes])
            bpart[n] = h
            bsend[i, n] = h.astype(BF16)
            branch_copy(i, n).start()
            return 0

        lax.fori_loop(0, 6, down_tile, 0)

    col192 = lax.broadcasted_iota(jnp.int32, (192, 256), 0) % 32

    def project(i):
        def merge_tile(n, _):
            lanes = pl.ds(pl.multiple_of(n * 256, 256), 256)
            branch_copy(i, n).wait()
            sc = sv[:, lanes].astype(F32)
            for h in range(2):
                rows = slice(128 * h, 128 * h + 128)
                base = fv[2 * h + i, :, :, lanes].reshape(128, 256).astype(F32)
                total = bpart[n, rows, :] + brecv[i, n, rows, :].astype(F32)
                bo[rows, lanes] = (base + sc * total).astype(BF16)
            return 0

        lax.fori_loop(0, 6, merge_tile, 0)

        def expand_tile(n, _):
            lanes = pl.ds(pl.multiple_of(n * 256, 256), 256)
            h = dot(bo[...], pev[:, lanes])
            hid[:, lanes] = jnp.maximum(h, 0.0).astype(BF16)
            return 0

        lax.fori_loop(0, 4, expand_tile, 0)

        acc[...] = jnp.zeros_like(acc)

        def tap(n, _):
            dy = n // 3
            dx = n % 3
            h = dot(hid[...], pkv[n])
            rows = pl.ds(pl.multiple_of((2 - dy) * 32, 32), 128)
            for k in range(2):
                acc[k, dx, rows, :] = acc[k, dx, rows, :] + h[128 * k : 128 * k + 128]
            return 0

        lax.fori_loop(0, 9, tap, 0)

        reg = lax.broadcasted_iota(jnp.int32, (REG, 192), 0)
        for k in range(2):
            img = 2 * k + i
            total = shifted(acc[k, 0], 1, col192) + acc[k, 1] + shifted(acc[k, 2], -1, col192)
            above = jnp.where(r > 0, rids[jnp.maximum(r - 1, 0), img, 3:4, :], -1)
            below = jnp.where(r < 7, rids[jnp.minimum(r + 1, 7), img, 0:1, :], -1)
            ids = jnp.concatenate(
                [above] + [rids[r, img, y : y + 1, :] for y in range(4)] + [below], axis=1
            )
            onehot = jnp.where(reg == ids, 1.0, 0.0).astype(BF16)
            hi, mid, lo = split3(total)
            pooled[64 * img : 64 * img + 64, :] = dot(onehot, hi) + dot(onehot, mid) + dot(onehot, lo)

    for copy in rid_copies:
        copy.wait()
    loads["rid"].wait()
    loads["gain"].wait()
    loads["scale"].wait()

    wait_halo(0)
    halo_part(0)
    layer_norm(0)
    norm_copy(0).start()
    loads["w1"].wait()
    loads["w2"].wait()

    for copy in key_rows:
        copy.wait()
    loads["key"].wait()
    half = pl.ds(b * 8 + 4 * s, 4)
    key_batch = [
        remote(kall.at[half], kall.at[half], ks2.at[d], kr2.at[d], batch_peer[d]) for d in range(7)
    ]
    for copy in key_batch:
        copy.start()

    norm_copy(0).wait()
    mlp(0)
    loads["pe"].wait()
    loads["pk"].wait()
    project(0)

    wait_halo(1)
    halo_part(1)
    layer_norm(1)
    norm_copy(1).start()
    for copy in key_batch:
        copy.wait()
    key_sib = []
    for d in range(1, 8):
        part = pl.ds(lax.rem(b + 8 - d, 8) * 8 + 4 * s, 4)
        key_sib.append(remote(kall.at[part], kall.at[part], ks3.at[d], kr3.at[d], sib))
    for copy in key_sib:
        copy.start()
    norm_copy(1).wait()
    mlp(1)
    project(1)

    loads["own"].wait()
    loads["par"].wait()
    place = lax.broadcasted_iota(jnp.int32, (256, 256), 0)
    perm = jnp.where(place == ownv[...], 1.0, 0.0).astype(BF16)
    hi, mid, lo = split3(pooled[...])
    ordered[...] = (dot(perm, hi) + dot(perm, mid) + dot(perm, lo)).reshape(8, 32, 256)
    pool_copies = [
        remote(ordered.at[lax.rem(r + d, 8)], gathered.at[d], ps.at[d], pr.at[d], row_peer[d - 1])
        for d in range(1, 8)
    ]
    for copy in pool_copies:
        copy.start()

    for copy in key_sib:
        copy.wait()

    ones = jnp.ones((8, 256), BF16)

    def key_norms(n, _):
        k = kall[pl.ds(n * 8, 8)].reshape(256, 256).astype(F32)
        sq = k * k
        top = sq.astype(BF16)
        bottom = (sq - top.astype(F32)).astype(BF16)
        total = dot_t(ones, top) + dot_t(ones, bottom)
        knorm[:, pl.ds(pl.multiple_of(n * 256, 256), 256)] = lax.rsqrt(total + NORM_EPS) * 10.0
        return 0

    lax.fori_loop(0, 8, key_norms, 0)

    slot = lax.broadcasted_iota(jnp.int32, (1, 256), 1)
    partner = jnp.concatenate([parv[k : k + 1, :] for k in range(4)], axis=1)
    positive = (slot // REG * REG + b * 256 + partner).astype(F32)
    used = jnp.zeros((1, 256), F32)
    for k in range(4):
        ids = jnp.max(rids[:, k].astype(F32), axis=0)
        most = jnp.max(jnp.max(ids, axis=1, keepdims=True), axis=0, keepdims=True)
        here = (slot // REG == k) & ((slot % REG).astype(F32) <= most)
        used = jnp.where(here, 1.0, used)
    mine = (lax.broadcasted_iota(jnp.int32, (32, 256), 0) + 32 * r) == ownv[...]
    pos = jnp.sum(jnp.where(mine, positive, 0.0), axis=1, keepdims=True)
    ok = jnp.sum(jnp.where(mine, used, 0.0), axis=1, keepdims=True)

    for copy in pool_copies:
        copy.wait()
    total = ordered[r]
    for d in range(1, 8):
        total = total + gathered[d]
    sibsum[0] = total
    sib_copy = remote(sibsum.at[0], sibsum.at[1], ss.at[0], sr.at[0], sib)
    sib_copy.start()
    sib_copy.wait()
    total = sibsum[0] + sibsum[1]
    probe = total * lax.rsqrt(jnp.sum(total * total, axis=1, keepdims=True) + NORM_EPS)
    emb_o[...] = probe
    hi, mid, lo = split3(probe)
    keys = kall[...].reshape(2048, 256)
    logits = (dot_t(hi, keys) + dot_t(mid, keys) + dot_t(lo, keys)) * knorm[0:1, :]
    sums = jnp.log(jnp.sum(jnp.exp(logits), axis=1, keepdims=True))
    index = lax.broadcasted_iota(jnp.int32, (32, 2048), 1).astype(F32)
    pos_logit = jnp.sum(jnp.where(index == pos, logits, 0.0), axis=1, keepdims=True)
    loss = jnp.where(ok > 0.5, sums - pos_logit, 0.0)
    eye = lax.broadcasted_iota(jnp.int32, (32, 32), 0) == lax.broadcasted_iota(jnp.int32, (32, 32), 1)
    loss_o[...] = jnp.sum(jnp.where(eye, loss, 0.0), axis=0, keepdims=True)


def body(*args):
    args = list(args)
    args[2] = args[2].reshape(1, -1)
    args[5] = args[5].reshape(1, -1)
    dma = pltpu.SemaphoreType.DMA
    vmem = pltpu.VMEM
    scratch = [
        vmem((4, 4, 32, 1536), BF16),
        vmem((2, 2, 3, 32, 1536), BF16),
        vmem((7, 7, 1536), BF16),
        vmem((7, 8, 1536), F32),
        vmem((1536, 1536), BF16),
        vmem((1536, 1536), BF16),
        vmem((1536, 1024), BF16),
        vmem((9, 1024, 256), BF16),
        vmem((1, 1536), BF16),
        vmem((1, 1536), BF16),
        vmem((1, 256), jnp.int32),
        vmem((4, 64), jnp.int32),
        vmem((2, 4, 32, 1536), F32),
        vmem((2, 2, 128, 1536), BF16),
        vmem((256, 1536), BF16),
        vmem((6, 256, 256), F32),
        vmem((2, 6, 256, 256), BF16),
        vmem((2, 6, 256, 256), BF16),
        vmem((256, 1536), BF16),
        vmem((256, 1024), BF16),
        vmem((2, 3, 192, 256), F32),
        vmem((256, 256), F32),
        vmem((8, 32, 256), F32),
        vmem((8, 32, 256), F32),
        vmem((2, 32, 256), F32),
        vmem((8, 4, 4, 32), jnp.int32),
        vmem((64, 32, 256), BF16),
        vmem((8, 2048), F32),
        dma((12,)),
        dma((2, 2)), dma((2, 2)),
        dma((2,)), dma((2,)),
        dma((2, 6)), dma((2, 6)),
        dma((8,)), dma((8,)),
        dma((8,)), dma((8,)),
        dma((8,)), dma((8,)),
        dma((8,)), dma((8,)),
        dma((8,)), dma((8,)),
        dma((1,)), dma((1,)),
    ]
    emb, loss = pl.pallas_call(
        kernel,
        out_shape=(
            jax.ShapeDtypeStruct((32, 256), F32),
            jax.ShapeDtypeStruct((1, 32), F32),
        ),
        in_specs=[pl.BlockSpec(memory_space=pl.ANY)] * 12,
        out_specs=(pl.BlockSpec(memory_space=pltpu.VMEM), pl.BlockSpec(memory_space=pltpu.VMEM)),
        scratch_shapes=scratch,
        compiler_params=pltpu.CompilerParams(
            collective_id=0, has_side_effects=True, vmem_limit_bytes=60 * 1024 * 1024
        ),
        name="region_loss",
    )(*args)
    return emb, loss.reshape(32)


def solution(mesh):
    in_specs = (
        P("batch", "rows", None, None),
        P(),
        P(),
        P(None, "section"),
        P("section", None),
        P(),
        P(None, "section"),
        P(None, "section", None),
        P("batch", "rows", None),
        P("batch", None),
        P("batch", None),
        P(("batch", "rows"), None),
    )
    out_specs = (P(("batch", "rows"), None), P(("batch", "rows")))
    return jax.shard_map(body, mesh=mesh, in_specs=in_specs, out_specs=out_specs, check_vma=False)
```

```python
import jax
import jax.numpy as jnp
from jax import lax
from jax.experimental import pallas as pl
from jax.experimental.pallas import tpu as pltpu
from jax.sharding import PartitionSpec as P

MESH = pl.DeviceIdType.MESH
REG = 64
LN_EPS = 1e-06
NORM_EPS = 1e-06
F32 = jnp.float32
BF16 = jnp.bfloat16


def split3(x):
    hi = x.astype(BF16)
    rest = x - hi.astype(F32)
    mid = rest.astype(BF16)
    lo = (rest - mid.astype(F32)).astype(BF16)
    return hi, mid, lo


def dot(a, b):
    return jnp.dot(a, b, preferred_element_type=F32)


def dot_t(a, b):
    return lax.dot_general(a, b, (((1,), (1,)), ((), ())), preferred_element_type=F32)


def gelu(x):
    return 0.5 * x * (1.0 + lax.erf(x * 0.7071067811865476))


def shifted(x, by, col):
    if by == 0:
        return x
    n = x.shape[0]
    moved = pltpu.roll(x, by % n, 0)
    keep = (col >= by) if by > 0 else (col < 32 + by)
    return jnp.where(keep, moved, 0.0)


def kernel(
    f, dwk, gain, w1, w2, scale, pe, pk, rid, own, par, key,
    emb_o, loss_o,
    fv, halo, dwv, dwf, w1v, w2v, pev, pkv, gv, sv, ownv, parv,
    taps, nrm, inner, bpart, bsend, brecv, bo, hid, acc, pooled, ordered, gathered, sibsum,
    rids, kall, knorm,
    lsem, hs, hr, ns, nr, bs, br, rs1, rr1, ks1, kr1, ks2, kr2, ks3, kr3, ps, pr, ss, sr,
):
    b = lax.axis_index("batch")
    r = lax.axis_index("rows")
    s = lax.axis_index("section")
    sib = (b, r, 1 - s)
    up = (b, jnp.maximum(r - 1, 0), s)
    down = (b, jnp.minimum(r + 1, 7), s)
    row_peer = [(b, lax.rem(r + d, 8), s) for d in range(1, 8)]
    batch_peer = [(lax.rem(b + d, 8), r, s) for d in range(1, 8)]

    barrier = pltpu.get_barrier_semaphore()
    for device in [sib] + row_peer + batch_peer:
        pl.semaphore_signal(barrier, inc=1, device_id=device, device_id_type=MESH)

    def local(src, dst, i):
        return pltpu.make_async_copy(src, dst, lsem.at[i])

    def remote(src, dst, send, recv, device):
        return pltpu.make_async_remote_copy(
            src_ref=src, dst_ref=dst, send_sem=send, recv_sem=recv, device_id=device, device_id_type=MESH
        )

    loads = {
        "f": local(f, fv, 0),
        "dw": local(dwk, dwv, 1),
        "rid": local(rid, rids.at[r], 2),
        "key": local(key, kall.at[b * 8 + r], 3),
        "own": local(own, ownv, 4),
        "par": local(par, parv, 5),
        "w1": local(w1, w1v, 6),
        "w2": local(w2, w2v, 7),
        "pe": local(pe, pev, 8),
        "pk": local(pk, pkv, 9),
        "gain": local(gain, gv, 10),
        "scale": local(scale, sv, 11),
    }
    for name in ("dw", "f", "gain", "scale", "rid", "key", "own", "par", "w1", "w2", "pe", "pk"):
        loads[name].start()

    pl.semaphore_wait(barrier, 15)

    def halo_up(i):
        return remote(f.at[2 * s + i, pl.ds(0, 3)], halo.at[i, 1], hs.at[i, 0], hr.at[i, 1], up)

    def halo_down(i):
        return remote(f.at[2 * s + i, pl.ds(1, 3)], halo.at[i, 0], hs.at[i, 1], hr.at[i, 0], down)

    def start_halo(i):
        @pl.when(r > 0)
        def _():
            halo_up(i).start()

        @pl.when(r < 7)
        def _():
            halo_down(i).start()

    def halo_sent(i):
        @pl.when(r > 0)
        def _():
            halo_up(i).wait_send()

        @pl.when(r < 7)
        def _():
            halo_down(i).wait_send()

    start_halo(0)

    rid_copies = [
        remote(rid, rids.at[r], rs1.at[d], rr1.at[d], row_peer[d]) for d in range(7)
    ]
    key_rows = [
        remote(key, kall.at[b * 8 + r], ks1.at[d], kr1.at[d], row_peer[d]) for d in range(7)
    ]
    for copy in rid_copies + key_rows:
        copy.start()

    for i in range(2):
        @pl.when(r == 0)
        def _():
            halo[i, 0] = jnp.zeros_like(halo[i, 0])

        @pl.when(r == 7)
        def _():
            halo[i, 1] = jnp.zeros_like(halo[i, 1])

    loads["dw"].wait()
    for dy in range(7):
        dwf[dy, 0:7, :] = dwv[dy].astype(F32)
    loads["f"].wait()

    col32 = lax.broadcasted_iota(jnp.int32, (32, 128), 0)

    def conv_rows(i, lanes, rows, get, first):
        for y in range(4):
            sums = [None] * 7
            for yi in rows:
                dy = yi - y + 3
                if dy < 0 or dy > 6:
                    continue
                x = get(yi)
                for dx in range(7):
                    term = x * dwf[dy, dx : dx + 1, lanes]
                    sums[dx] = term if sums[dx] is None else sums[dx] + term
            total = sums[3]
            for dx in (0, 1, 2, 4, 5, 6):
                total = total + shifted(sums[dx], 3 - dx, col32)
            if first:
                taps[i, y, :, lanes] = total
            else:
                taps[i, y, :, lanes] = taps[i, y, :, lanes] + total

    def own_part(n, _):
        i = n // 12
        lanes = pl.ds(pl.multiple_of((n % 12) * 128, 128), 128)
        xs = [fv[2 * s + i, y, :, lanes].astype(F32) for y in range(4)]
        conv_rows(i, lanes, range(4), lambda yi: xs[yi], True)
        return 0

    lax.fori_loop(0, 24, own_part, 0)
    halo_sent(0)
    start_halo(1)

    def halo_part(i):
        def step(n, _):
            lanes = pl.ds(pl.multiple_of(n * 128, 128), 128)
            xs = {}
            for k in range(3):
                xs[k - 3] = halo[i, 0, k, :, lanes].astype(F32)
                xs[4 + k] = halo[i, 1, k, :, lanes].astype(F32)
            conv_rows(i, lanes, (-3, -2, -1, 4, 5, 6), lambda yi: xs[yi], False)
            return 0

        lax.fori_loop(0, 12, step, 0)

    def layer_norm(i):
        def step(y, _):
            t = taps[i, y]
            mean = jnp.sum(t, axis=-1, keepdims=True) * (1.0 / 1536)
            t = t - mean
            spread = jnp.sum(t * t, axis=-1, keepdims=True) * (1.0 / 1536)
            out = t * lax.rsqrt(spread + LN_EPS) * gv[...].astype(F32).reshape(1, 1536)
            nrm[i, s, pl.ds(pl.multiple_of(y * 32, 32), 32), :] = out.astype(BF16)
            return 0

        lax.fori_loop(0, 4, step, 0)

    def norm_copy(i):
        return remote(nrm.at[i, s], nrm.at[i, s], ns.at[i], nr.at[i], sib)

    def branch_copy(i, half):
        part = pl.ds(3 * half, 3)
        return remote(bsend.at[i, part], brecv.at[i, part], bs.at[i, half], br.at[i, half], sib)

    def wait_halo(i):
        @pl.when(r > 0)
        def _():
            halo_down(i).wait_recv()

        @pl.when(r < 7)
        def _():
            halo_up(i).wait_recv()

    def tile(n):
        return slice(256 * n, 256 * n + 256)

    def mlp(i):
        x = nrm[i].reshape(256, 1536)
        for n in range(6):
            inner[:, tile(n)] = gelu(dot(x, w1v[:, tile(n)])).astype(BF16)
        for half in range(2):
            for n in range(3 * half, 3 * half + 3):
                h = dot(inner[...], w2v[:, tile(n)])
                bpart[n] = h
                bsend[i, n] = h.astype(BF16)
            branch_copy(i, half).start()

    col192 = lax.broadcasted_iota(jnp.int32, (192, 256), 0) % 32

    def merge(i):
        def merge_tile(n, _):
            lanes = pl.ds(pl.multiple_of(n * 256, 256), 256)
            sc = sv[lanes].astype(F32).reshape(1, 256)
            for h in range(2):
                rows = slice(128 * h, 128 * h + 128)
                base = fv[2 * h + i, :, :, lanes].reshape(128, 256).astype(F32)
                total = bpart[n, rows, :] + brecv[i, n, rows, :].astype(F32)
                bo[rows, lanes] = (base + sc * total).astype(BF16)
            return 0

        for half in range(2):
            branch_copy(i, half).wait()
            lax.fori_loop(3 * half, 3 * half + 3, merge_tile, 0)

    def expand(i):
        for n in range(4):
            hid[:, tile(n)] = jnp.maximum(dot(bo[...], pev[:, tile(n)]), 0.0).astype(BF16)

    def project(i):
        acc[...] = jnp.zeros_like(acc)
        for n in range(9):
            dy, dx = divmod(n, 3)
            h = dot(hid[...], pkv[n])
            rows = slice((2 - dy) * 32, (2 - dy) * 32 + 128)
            for k in range(2):
                acc[k, dx, rows, :] = acc[k, dx, rows, :] + h[128 * k : 128 * k + 128]

        reg = lax.broadcasted_iota(jnp.int32, (REG, 192), 0)
        for k in range(2):
            img = 2 * k + i
            total = shifted(acc[k, 0], 1, col192) + acc[k, 1] + shifted(acc[k, 2], -1, col192)
            above = jnp.where(r > 0, rids[jnp.maximum(r - 1, 0), img, 3:4, :], -1)
            below = jnp.where(r < 7, rids[jnp.minimum(r + 1, 7), img, 0:1, :], -1)
            ids = jnp.concatenate(
                [above] + [rids[r, img, y : y + 1, :] for y in range(4)] + [below], axis=1
            )
            onehot = jnp.where(reg == ids, 1.0, 0.0).astype(BF16)
            hi, mid, lo = split3(total)
            pooled[64 * img : 64 * img + 64, :] = dot(onehot, hi) + dot(onehot, mid) + dot(onehot, lo)

    for copy in rid_copies:
        copy.wait()
    loads["rid"].wait()
    loads["gain"].wait()
    loads["scale"].wait()

    wait_halo(0)
    halo_part(0)
    layer_norm(0)
    norm_copy(0).start()
    loads["w1"].wait()
    loads["w2"].wait()

    for copy in key_rows:
        copy.wait()
    loads["key"].wait()
    half = pl.ds(b * 8 + 4 * s, 4)
    key_batch = [
        remote(kall.at[half], kall.at[half], ks2.at[d], kr2.at[d], batch_peer[d]) for d in range(7)
    ]
    for copy in key_batch:
        copy.start()

    norm_copy(0).wait()
    mlp(0)

    wait_halo(1)
    halo_sent(1)
    halo_part(1)
    layer_norm(1)
    norm_copy(1).start()
    loads["pe"].wait()
    loads["pk"].wait()
    merge(0)
    expand(0)
    norm_copy(1).wait()
    mlp(1)
    project(0)
    for copy in key_batch:
        copy.wait()
    key_sib = []
    for d in range(1, 8):
        part = pl.ds(lax.rem(b + 8 - d, 8) * 8 + 4 * s, 4)
        key_sib.append(remote(kall.at[part], kall.at[part], ks3.at[d], kr3.at[d], sib))
    merge(1)
    for copy in key_sib:
        copy.start()
    expand(1)
    project(1)

    loads["own"].wait()
    loads["par"].wait()
    place = lax.broadcasted_iota(jnp.int32, (256, 256), 0)
    perm = jnp.where(place == ownv[...], 1.0, 0.0).astype(BF16)
    hi, mid, lo = split3(pooled[...])
    ordered[...] = (dot(perm, hi) + dot(perm, mid) + dot(perm, lo)).reshape(8, 32, 256)
    pool_copies = [
        remote(ordered.at[lax.rem(r + d, 8)], gathered.at[d], ps.at[d], pr.at[d], row_peer[d - 1])
        for d in range(1, 8)
    ]
    for copy in pool_copies:
        copy.start()

    for copy in key_sib:
        copy.wait()

    ones = jnp.ones((8, 256), BF16)

    def key_norms(n, _):
        k = kall[pl.ds(n * 8, 8)].reshape(256, 256).astype(F32)
        sq = k * k
        top = sq.astype(BF16)
        bottom = (sq - top.astype(F32)).astype(BF16)
        total = dot_t(ones, top) + dot_t(ones, bottom)
        knorm[:, pl.ds(pl.multiple_of(n * 256, 256), 256)] = lax.rsqrt(total + NORM_EPS) * 10.0
        return 0

    lax.fori_loop(0, 8, key_norms, 0)

    slot = lax.broadcasted_iota(jnp.int32, (1, 256), 1)
    partner = jnp.concatenate([parv[k : k + 1, :] for k in range(4)], axis=1)
    positive = (slot // REG * REG + b * 256 + partner).astype(F32)
    used = jnp.zeros((1, 256), F32)
    for k in range(4):
        ids = jnp.max(rids[:, k].astype(F32), axis=0)
        most = jnp.max(jnp.max(ids, axis=1, keepdims=True), axis=0, keepdims=True)
        here = (slot // REG == k) & ((slot % REG).astype(F32) <= most)
        used = jnp.where(here, 1.0, used)
    mine = (lax.broadcasted_iota(jnp.int32, (32, 256), 0) + 32 * r) == ownv[...]
    pos = jnp.sum(jnp.where(mine, positive, 0.0), axis=1, keepdims=True)
    ok = jnp.sum(jnp.where(mine, used, 0.0), axis=1, keepdims=True)

    for copy in pool_copies:
        copy.wait()
    total = ordered[r]
    for d in range(1, 8):
        total = total + gathered[d]
    sibsum[0] = total
    sib_copy = remote(sibsum.at[0], sibsum.at[1], ss.at[0], sr.at[0], sib)
    sib_copy.start()
    sib_copy.wait()
    total = sibsum[0] + sibsum[1]
    probe = total * lax.rsqrt(jnp.sum(total * total, axis=1, keepdims=True) + NORM_EPS)
    emb_o[...] = probe
    hi, mid, lo = split3(probe)
    keys = kall[...].reshape(2048, 256)
    parts = dot_t(jnp.concatenate([hi, mid, lo], axis=0), keys)
    logits = (parts[0:32] + parts[32:64] + parts[64:96]) * knorm[0:1, :]
    sums = jnp.log(jnp.sum(jnp.exp(logits), axis=1, keepdims=True))
    index = lax.broadcasted_iota(jnp.int32, (32, 2048), 1).astype(F32)
    pos_logit = jnp.sum(jnp.where(index == pos, logits, 0.0), axis=1, keepdims=True)
    loss = jnp.where(ok > 0.5, sums - pos_logit, 0.0)
    eye = lax.broadcasted_iota(jnp.int32, (32, 32), 0) == lax.broadcasted_iota(jnp.int32, (32, 32), 1)
    loss_o[...] = jnp.sum(jnp.where(eye, loss, 0.0), axis=0, keepdims=True)


def finish(emb, loss, emb_o, loss_o):
    emb_o[...] = emb[...]
    loss_o[...] = loss[...]


def body(*args):
    dma = pltpu.SemaphoreType.DMA
    vmem = pltpu.VMEM
    scratch = [
        vmem((4, 4, 32, 1536), BF16),
        vmem((2, 2, 3, 32, 1536), BF16),
        vmem((7, 7, 1536), BF16),
        vmem((7, 8, 1536), F32),
        vmem((1536, 1536), BF16),
        vmem((1536, 1536), BF16),
        vmem((1536, 1024), BF16),
        vmem((9, 1024, 256), BF16),
        vmem((1536,), BF16),
        vmem((1536,), BF16),
        vmem((1, 256), jnp.int32),
        vmem((4, 64), jnp.int32),
        vmem((2, 4, 32, 1536), F32),
        vmem((2, 2, 128, 1536), BF16),
        vmem((256, 1536), BF16),
        vmem((6, 256, 256), F32),
        vmem((2, 6, 256, 256), BF16),
        vmem((2, 6, 256, 256), BF16),
        vmem((256, 1536), BF16),
        vmem((256, 1024), BF16),
        vmem((2, 3, 192, 256), F32),
        vmem((256, 256), F32),
        vmem((8, 32, 256), F32),
        vmem((8, 32, 256), F32),
        vmem((2, 32, 256), F32),
        vmem((8, 4, 4, 32), jnp.int32),
        vmem((64, 32, 256), BF16),
        vmem((8, 2048), F32),
        dma((12,)),
        dma((2, 2)), dma((2, 2)),
        dma((2,)), dma((2,)),
        dma((2, 2)), dma((2, 2)),
        dma((8,)), dma((8,)),
        dma((8,)), dma((8,)),
        dma((8,)), dma((8,)),
        dma((8,)), dma((8,)),
        dma((8,)), dma((8,)),
        dma((1,)), dma((1,)),
    ]
    emb, loss = pl.pallas_call(
        kernel,
        out_shape=(
            jax.ShapeDtypeStruct((32, 256), F32),
            jax.ShapeDtypeStruct((1, 32), F32),
        ),
        in_specs=[pl.BlockSpec(memory_space=pl.ANY)] * 12,
        out_specs=(pl.BlockSpec(memory_space=pltpu.VMEM), pl.BlockSpec(memory_space=pltpu.VMEM)),
        scratch_shapes=scratch,
        compiler_params=pltpu.CompilerParams(
            collective_id=0, has_side_effects=True, vmem_limit_bytes=60 * 1024 * 1024
        ),
        name="region_loss",
    )(*args)
    emb, loss = pl.pallas_call(
        finish,
        out_shape=(
            jax.ShapeDtypeStruct((32, 256), F32),
            jax.ShapeDtypeStruct((1, 32), F32),
        ),
        in_specs=[pl.BlockSpec(memory_space=pltpu.VMEM)] * 2,
        out_specs=(pl.BlockSpec(memory_space=pltpu.VMEM), pl.BlockSpec(memory_space=pltpu.VMEM)),
        name="finish",
    )(emb, loss)
    return emb, loss.reshape(32)


def solution(mesh):
    in_specs = (
        P("batch", "rows", None, None),
        P(),
        P(),
        P(None, "section"),
        P("section", None),
        P(),
        P(None, "section"),
        P(None, "section", None),
        P("batch", "rows", None),
        P("batch", None),
        P("batch", None),
        P(("batch", "rows"), None),
    )
    out_specs = (P(("batch", "rows"), None), P(("batch", "rows")))
    return jax.shard_map(body, mesh=mesh, in_specs=in_specs, out_specs=out_specs, check_vma=False)
```

```python
import jax
import jax.numpy as jnp
from jax import lax
from jax.experimental import pallas as pl
from jax.experimental.pallas import tpu as pltpu
from jax.sharding import PartitionSpec as P

MESH = pl.DeviceIdType.MESH
REG = 64
LN_EPS = 1e-06
NORM_EPS = 1e-06
F32 = jnp.float32
BF16 = jnp.bfloat16


def split3(x):
    hi = x.astype(BF16)
    rest = x - hi.astype(F32)
    mid = rest.astype(BF16)
    lo = (rest - mid.astype(F32)).astype(BF16)
    return hi, mid, lo


def dot(a, b):
    return jnp.dot(a, b, preferred_element_type=F32)


def dot_t(a, b):
    return lax.dot_general(a, b, (((1,), (1,)), ((), ())), preferred_element_type=F32)


def gelu(x):
    return 0.5 * x * (1.0 + lax.erf(x * 0.7071067811865476))


def shifted(x, by, col):
    if by == 0:
        return x
    n = x.shape[0]
    moved = pltpu.roll(x, by % n, 0)
    keep = (col >= by) if by > 0 else (col < 32 + by)
    return jnp.where(keep, moved, 0.0)


def kernel(
    f, dwk, gain, w1, w2, scale, pe, pk, rid, own, par, key,
    emb_o, loss_o,
    fv, halo, dwv, dwf, w1v, w2v, pev, pkv, gv, sv, ownv, parv,
    taps, nrm, inner, bpart, bsend, brecv, bo, hid, acc, spot, ordered, ordered16, gathered,
    rids, kall, knorm,
    lsem, hs, hr, ns, nr, bs, br, rs1, rr1, ks1, kr1, ks2, kr2, ks3, kr3, ps, pr,
):
    b = lax.axis_index("batch")
    r = lax.axis_index("rows")
    s = lax.axis_index("section")
    sib = (b, r, 1 - s)
    up = (b, jnp.maximum(r - 1, 0), s)
    down = (b, jnp.minimum(r + 1, 7), s)
    row_peer = [(b, lax.rem(r + d, 8), s) for d in range(1, 8)]
    cross_peer = [(b, lax.rem(r + d, 8), 1 - s) for d in range(1, 8)]
    batch_peer = [(lax.rem(b + d, 8), r, s) for d in range(1, 8)]

    barrier = pltpu.get_barrier_semaphore()
    for device in [sib] + row_peer + cross_peer + batch_peer:
        pl.semaphore_signal(barrier, inc=1, device_id=device, device_id_type=MESH)

    def local(src, dst, i):
        return pltpu.make_async_copy(src, dst, lsem.at[i])

    def remote(src, dst, send, recv, device):
        return pltpu.make_async_remote_copy(
            src_ref=src, dst_ref=dst, send_sem=send, recv_sem=recv, device_id=device, device_id_type=MESH
        )

    loads = {
        "f": local(f, fv, 0),
        "dw": local(dwk, dwv, 1),
        "rid": local(rid, rids.at[r], 2),
        "key": local(key, kall.at[b * 8 + r], 3),
        "own": local(own, ownv, 4),
        "par": local(par, parv, 5),
        "w1": local(w1, w1v, 6),
        "w2": local(w2, w2v, 7),
        "pe": local(pe, pev, 8),
        "pk": local(pk, pkv, 9),
        "gain": local(gain, gv, 10),
        "scale": local(scale, sv, 11),
    }
    for name in ("dw", "f", "gain", "scale", "rid", "key", "own", "par", "w1", "w2", "pe", "pk"):
        loads[name].start()

    pl.semaphore_wait(barrier, 22)

    def halo_up(i, h):
        lanes = pl.ds(768 * h, 768)
        return remote(
            f.at[2 * s + i, pl.ds(0, 3), :, lanes], halo.at[i, 1, :, :, lanes],
            hs.at[i, 0, h], hr.at[i, 1, h], up,
        )

    def halo_down(i, h):
        lanes = pl.ds(768 * h, 768)
        return remote(
            f.at[2 * s + i, pl.ds(1, 3), :, lanes], halo.at[i, 0, :, :, lanes],
            hs.at[i, 1, h], hr.at[i, 0, h], down,
        )

    def start_halo(i, h):
        @pl.when(r > 0)
        def _():
            halo_up(i, h).start()

        @pl.when(r < 7)
        def _():
            halo_down(i, h).start()

    def halo_sent(i, h):
        @pl.when(r > 0)
        def _():
            halo_up(i, h).wait_send()

        @pl.when(r < 7)
        def _():
            halo_down(i, h).wait_send()

    start_halo(0, 0)
    rid_copies = [
        remote(rid, rids.at[r], rs1.at[d], rr1.at[d], row_peer[d]) for d in range(7)
    ]
    key_rows = [
        remote(key, kall.at[b * 8 + r], ks1.at[d], kr1.at[d], row_peer[d]) for d in range(7)
    ]
    for i in range(2):
        @pl.when(r == 0)
        def _():
            halo[i, 0] = jnp.zeros_like(halo[i, 0])

        @pl.when(r == 7)
        def _():
            halo[i, 1] = jnp.zeros_like(halo[i, 1])

    loads["dw"].wait()
    for dy in range(7):
        dwf[dy, 0:7, :] = dwv[dy].astype(F32)
    loads["f"].wait()

    col32 = lax.broadcasted_iota(jnp.int32, (32, 128), 0)

    def conv_rows(i, lanes, rows, get, first):
        for y in range(4):
            sums = [None] * 7
            for yi in rows:
                dy = yi - y + 3
                if dy < 0 or dy > 6:
                    continue
                x = get(yi)
                for dx in range(7):
                    term = x * dwf[dy, dx : dx + 1, lanes]
                    sums[dx] = term if sums[dx] is None else sums[dx] + term
            total = sums[3]
            for dx in (0, 1, 2, 4, 5, 6):
                total = total + shifted(sums[dx], 3 - dx, col32)
            if first:
                taps[i, y, :, lanes] = total
            else:
                taps[i, y, :, lanes] = taps[i, y, :, lanes] + total

    def own_part(n, _):
        i = n // 12
        lanes = pl.ds(pl.multiple_of((n % 12) * 128, 128), 128)
        xs = [fv[2 * s + i, y, :, lanes].astype(F32) for y in range(4)]
        conv_rows(i, lanes, range(4), lambda yi: xs[yi], True)
        return 0

    lax.fori_loop(0, 12, own_part, 0)
    start_halo(0, 1)
    lax.fori_loop(12, 24, own_part, 0)

    def halo_part(i, part):
        def step(n, _):
            lanes = pl.ds(pl.multiple_of(n * 128, 128), 128)
            xs = {}
            for k in range(3):
                xs[k - 3] = halo[i, 0, k, :, lanes].astype(F32)
                xs[4 + k] = halo[i, 1, k, :, lanes].astype(F32)
            conv_rows(i, lanes, (-3, -2, -1, 4, 5, 6), lambda yi: xs[yi], False)
            return 0

        lax.fori_loop(6 * part, 6 * part + 6, step, 0)

    def layer_norm(i):
        def step(y, _):
            t = taps[i, y]
            mean = jnp.sum(t, axis=-1, keepdims=True) * (1.0 / 1536)
            t = t - mean
            spread = jnp.sum(t * t, axis=-1, keepdims=True) * (1.0 / 1536)
            out = t * lax.rsqrt(spread + LN_EPS) * gv[...].astype(F32).reshape(1, 1536)
            nrm[i, s, pl.ds(pl.multiple_of(y * 32, 32), 32), :] = out.astype(BF16)
            return 0

        for part in range(2):
            lax.fori_loop(2 * part, 2 * part + 2, step, 0)
            norm_copy(i, part).start()

    def norm_copy(i, part):
        rows = nrm.at[i, s, pl.ds(64 * part, 64)]
        return remote(rows, rows, ns.at[i, part], nr.at[i, part], sib)

    def branch_copy(i, half):
        part = pl.ds(3 * half, 3)
        return remote(bsend.at[i, part], brecv.at[i, part], bs.at[i, half], br.at[i, half], sib)

    def wait_halo(i, h):
        @pl.when(r > 0)
        def _():
            halo_down(i, h).wait_recv()

        @pl.when(r < 7)
        def _():
            halo_up(i, h).wait_recv()

    def tile(n):
        return slice(256 * n, 256 * n + 256)

    def mlp(i):
        x = nrm[i].reshape(256, 1536)
        for n in range(6):
            inner[:, tile(n)] = gelu(dot(x, w1v[:, tile(n)])).astype(BF16)
        for half in range(2):
            for n in range(3 * half, 3 * half + 3):
                h = dot(inner[...], w2v[:, tile(n)])
                bpart[n] = h
                bsend[i, n] = h.astype(BF16)
            branch_copy(i, half).start()

    col192 = lax.broadcasted_iota(jnp.int32, (192, 256), 0) % 32

    def merge(i):
        def merge_tile(n, _):
            lanes = pl.ds(pl.multiple_of(n * 256, 256), 256)
            sc = sv[lanes].astype(F32).reshape(1, 256)
            for h in range(2):
                rows = slice(128 * h, 128 * h + 128)
                base = fv[2 * h + i, :, :, lanes].reshape(128, 256).astype(F32)
                total = bpart[n, rows, :] + brecv[i, n, rows, :].astype(F32)
                bo[rows, lanes] = (base + sc * total).astype(BF16)
            return 0

        for half in range(2):
            branch_copy(i, half).wait()
            lax.fori_loop(3 * half, 3 * half + 3, merge_tile, 0)

    def expand(i):
        for n in range(4):
            hid[:, tile(n)] = jnp.maximum(dot(bo[...], pev[:, tile(n)]), 0.0).astype(BF16)

    def project(i):
        acc[...] = jnp.zeros_like(acc)
        for n in range(9):
            dy, dx = divmod(n, 3)
            h = dot(hid[...], pkv[n])
            rows = slice((2 - dy) * 32, (2 - dy) * 32 + 128)
            for k in range(2):
                acc[k, dx, rows, :] = acc[k, dx, rows, :] + h[128 * k : 128 * k + 128]

        out = None
        for k in range(2):
            total = shifted(acc[k, 0], 1, col192) + acc[k, 1] + shifted(acc[k, 2], -1, col192)
            total = jnp.concatenate([total, jnp.zeros((64, 256), F32)], axis=0)
            for part in split3(total):
                term = dot(spot[2 * k + i], part)
                out = term if out is None else out + term
        if i == 0:
            ordered[...] = out.reshape(8, 32, 256)
        else:
            ordered[...] = ordered[...] + out.reshape(8, 32, 256)

    wait_halo(0, 0)
    halo_part(0, 0)
    halo_sent(0, 0)
    halo_sent(0, 1)
    for copy in rid_copies:
        copy.start()
    start_halo(1, 0)
    loads["gain"].wait()
    loads["scale"].wait()
    wait_halo(0, 1)
    halo_part(0, 1)
    start_halo(1, 1)
    for copy in key_rows:
        copy.start()
    layer_norm(0)
    loads["w1"].wait()
    loads["w2"].wait()

    for part in range(2):
        norm_copy(0, part).wait()
    mlp(0)

    for copy in rid_copies:
        copy.wait()
    for name in ("rid", "own", "par"):
        loads[name].wait()
    place = lax.broadcasted_iota(jnp.int32, (256, REG), 0)
    reg = lax.broadcasted_iota(jnp.int32, (REG, 256), 0)
    for img in range(4):
        above = jnp.where(r > 0, rids[jnp.maximum(r - 1, 0), img, 3:4, :], -1)
        below = jnp.where(r < 7, rids[jnp.minimum(r + 1, 7), img, 0:1, :], -1)
        rest = jnp.full((1, 64), -1, jnp.int32)
        ids = jnp.concatenate(
            [above] + [rids[r, img, y : y + 1, :] for y in range(4)] + [below, rest], axis=1
        )
        onehot = jnp.where(reg == ids, 1.0, 0.0).astype(BF16)
        perm = jnp.where(place == ownv[:, REG * img : REG * img + REG], 1.0, 0.0).astype(BF16)
        spot[img] = dot(perm, onehot).astype(BF16)

    wait_halo(1, 0)
    halo_part(1, 0)
    wait_halo(1, 1)
    halo_part(1, 1)
    layer_norm(1)
    halo_sent(1, 0)
    halo_sent(1, 1)
    loads["pe"].wait()
    loads["pk"].wait()
    merge(0)
    expand(0)
    for part in range(2):
        norm_copy(1, part).wait()
    mlp(1)
    for copy in key_rows:
        copy.wait()
    loads["key"].wait()
    half = pl.ds(b * 8 + 4 * s, 4)
    key_batch = [
        remote(kall.at[half], kall.at[half], ks2.at[d], kr2.at[d], batch_peer[d]) for d in range(7)
    ]
    for copy in key_batch:
        copy.start()
    project(0)
    merge(1)
    expand(1)
    project(1)

    ordered16[...] = ordered[...].astype(BF16)
    pool_copies = []
    for d in (2, 6, 3, 5, 1, 7, 4):
        block = ordered16.at[lax.rem(r + d, 8)]
        pool_copies.append(remote(block, gathered.at[0, d], ps.at[0, d], pr.at[0, d], row_peer[d - 1]))
        pool_copies.append(remote(block, gathered.at[1, d], ps.at[1, d], pr.at[1, d], cross_peer[d - 1]))
    pool_copies.append(remote(ordered16.at[r], gathered.at[1, 0], ps.at[1, 0], pr.at[1, 0], sib))
    for copy in pool_copies:
        copy.start()

    for copy in key_batch:
        copy.wait()
    key_sib = []
    for d in range(1, 8):
        part = pl.ds(lax.rem(b + 8 - d, 8) * 8 + 4 * s, 4)
        key_sib.append(remote(kall.at[part], kall.at[part], ks3.at[d], kr3.at[d], sib))
    for copy in key_sib:
        copy.start()

    for copy in key_sib:
        copy.wait()

    ones = jnp.ones((8, 256), BF16)

    def key_norms(n, _):
        k = kall[pl.ds(n * 8, 8)].reshape(256, 256).astype(F32)
        sq = k * k
        top = sq.astype(BF16)
        bottom = (sq - top.astype(F32)).astype(BF16)
        total = dot_t(ones, top) + dot_t(ones, bottom)
        knorm[:, pl.ds(pl.multiple_of(n * 256, 256), 256)] = lax.rsqrt(total + NORM_EPS) * 10.0
        return 0

    lax.fori_loop(0, 8, key_norms, 0)

    slot = lax.broadcasted_iota(jnp.int32, (1, 256), 1)
    partner = jnp.concatenate([parv[k : k + 1, :] for k in range(4)], axis=1)
    positive = (slot // REG * REG + b * 256 + partner).astype(F32)
    used = jnp.zeros((1, 256), F32)
    for k in range(4):
        ids = jnp.max(rids[:, k].astype(F32), axis=0)
        most = jnp.max(jnp.max(ids, axis=1, keepdims=True), axis=0, keepdims=True)
        here = (slot // REG == k) & ((slot % REG).astype(F32) <= most)
        used = jnp.where(here, 1.0, used)
    mine = (lax.broadcasted_iota(jnp.int32, (32, 256), 0) + 32 * r) == ownv[...]
    pos = jnp.sum(jnp.where(mine, positive, 0.0), axis=1, keepdims=True)
    ok = jnp.sum(jnp.where(mine, used, 0.0), axis=1, keepdims=True)

    for copy in pool_copies:
        copy.wait()
    same = ordered16[r].astype(F32)
    cross = gathered[1, 0].astype(F32)
    for d in range(1, 8):
        same = same + gathered[0, d].astype(F32)
        cross = cross + gathered[1, d].astype(F32)
    total = same + cross
    probe = total * lax.rsqrt(jnp.sum(total * total, axis=1, keepdims=True) + NORM_EPS)
    emb_o[...] = probe
    hi, mid, lo = split3(probe)
    keys = kall[...].reshape(2048, 256)
    parts = dot_t(jnp.concatenate([hi, mid, lo], axis=0), keys)
    logits = (parts[0:32] + parts[32:64] + parts[64:96]) * knorm[0:1, :]
    sums = jnp.log(jnp.sum(jnp.exp(logits), axis=1, keepdims=True))
    index = lax.broadcasted_iota(jnp.int32, (32, 2048), 1).astype(F32)
    pos_logit = jnp.sum(jnp.where(index == pos, logits, 0.0), axis=1, keepdims=True)
    loss = jnp.where(ok > 0.5, sums - pos_logit, 0.0)
    eye = lax.broadcasted_iota(jnp.int32, (32, 32), 0) == lax.broadcasted_iota(jnp.int32, (32, 32), 1)
    loss_o[...] = jnp.sum(jnp.where(eye, loss, 0.0), axis=0, keepdims=True)


def finish(emb, loss, emb_o, loss_o):
    emb_o[...] = emb[...]
    loss_o[...] = loss[...]


def body(*args):
    dma = pltpu.SemaphoreType.DMA
    vmem = pltpu.VMEM
    scratch = [
        vmem((4, 4, 32, 1536), BF16),
        vmem((2, 2, 3, 32, 1536), BF16),
        vmem((7, 7, 1536), BF16),
        vmem((7, 8, 1536), F32),
        vmem((1536, 1536), BF16),
        vmem((1536, 1536), BF16),
        vmem((1536, 1024), BF16),
        vmem((9, 1024, 256), BF16),
        vmem((1536,), BF16),
        vmem((1536,), BF16),
        vmem((1, 256), jnp.int32),
        vmem((4, 64), jnp.int32),
        vmem((2, 4, 32, 1536), F32),
        vmem((2, 2, 128, 1536), BF16),
        vmem((256, 1536), BF16),
        vmem((6, 256, 256), F32),
        vmem((2, 6, 256, 256), BF16),
        vmem((2, 6, 256, 256), BF16),
        vmem((256, 1536), BF16),
        vmem((256, 1024), BF16),
        vmem((2, 3, 192, 256), F32),
        vmem((4, 256, 256), BF16),
        vmem((8, 32, 256), F32),
        vmem((8, 32, 256), BF16),
        vmem((2, 8, 32, 256), BF16),
        vmem((8, 4, 4, 32), jnp.int32),
        vmem((64, 32, 256), BF16),
        vmem((8, 2048), F32),
        dma((12,)),
        dma((2, 2, 2)), dma((2, 2, 2)),
        dma((2, 2)), dma((2, 2)),
        dma((2, 2)), dma((2, 2)),
        dma((8,)), dma((8,)),
        dma((8,)), dma((8,)),
        dma((8,)), dma((8,)),
        dma((8,)), dma((8,)),
        dma((2, 8)), dma((2, 8)),
    ]
    emb, loss = pl.pallas_call(
        kernel,
        out_shape=(
            jax.ShapeDtypeStruct((32, 256), F32),
            jax.ShapeDtypeStruct((1, 32), F32),
        ),
        in_specs=[pl.BlockSpec(memory_space=pl.ANY)] * 12,
        out_specs=(pl.BlockSpec(memory_space=pltpu.VMEM), pl.BlockSpec(memory_space=pltpu.VMEM)),
        scratch_shapes=scratch,
        compiler_params=pltpu.CompilerParams(
            collective_id=0, has_side_effects=True, vmem_limit_bytes=60 * 1024 * 1024
        ),
        name="region_loss",
    )(*args)
    emb, loss = pl.pallas_call(
        finish,
        out_shape=(
            jax.ShapeDtypeStruct((32, 256), F32),
            jax.ShapeDtypeStruct((1, 32), F32),
        ),
        in_specs=[pl.BlockSpec(memory_space=pltpu.VMEM)] * 2,
        out_specs=(pl.BlockSpec(memory_space=pltpu.VMEM), pl.BlockSpec(memory_space=pltpu.VMEM)),
        name="finish",
    )(emb, loss)
    return emb, loss.reshape(32)


def solution(mesh):
    in_specs = (
        P("batch", "rows", None, None),
        P(),
        P(),
        P(None, "section"),
        P("section", None),
        P(),
        P(None, "section"),
        P(None, "section", None),
        P("batch", "rows", None),
        P("batch", None),
        P("batch", None),
        P(("batch", "rows"), None),
    )
    out_specs = (P(("batch", "rows"), None), P(("batch", "rows")))
    return jax.shard_map(body, mesh=mesh, in_specs=in_specs, out_specs=out_specs, check_vma=False)
```

```python
import jax
import jax.numpy as jnp
from jax import lax
from jax.experimental import pallas as pl
from jax.experimental.pallas import tpu as pltpu
from jax.sharding import PartitionSpec as P

MESH = pl.DeviceIdType.MESH
REG = 64
LN_EPS = 1e-06
NORM_EPS = 1e-06
F32 = jnp.float32
BF16 = jnp.bfloat16


def split3(x):
    hi = x.astype(BF16)
    rest = x - hi.astype(F32)
    mid = rest.astype(BF16)
    lo = (rest - mid.astype(F32)).astype(BF16)
    return hi, mid, lo


def dot(a, b):
    return jnp.dot(a, b, preferred_element_type=F32)


def dot_t(a, b):
    return lax.dot_general(a, b, (((1,), (1,)), ((), ())), preferred_element_type=F32)


def gelu(x):
    return 0.5 * x * (1.0 + lax.erf(x * 0.7071067811865476))


def shifted(x, by, col):
    if by == 0:
        return x
    n = x.shape[0]
    moved = pltpu.roll(x, by % n, 0)
    keep = (col >= by) if by > 0 else (col < 32 + by)
    return jnp.where(keep, moved, 0.0)


def kernel(
    f, dwk, gain, w1, w2, scale, pe, pk, rid, own, par, key,
    emb_o, loss_o,
    fv, halo, dwv, dwf, w1v, w2v, pev, pkv, gv, sv, ownv, parv,
    taps, nrm, inner, bpart, bsend, brecv, bo, hid, acc, spot, ordered, ordered16, gathered,
    rids, kall, knorm,
    lsem, hs, hr, ns, nr, bs, br, rs1, rr1, ks1, kr1, ks2, kr2, kzs, kzr, ks3, kr3, ps, pr,
):
    b = lax.axis_index("batch")
    r = lax.axis_index("rows")
    s = lax.axis_index("section")
    sib = (b, r, 1 - s)
    up = (b, jnp.maximum(r - 1, 0), s)
    down = (b, jnp.minimum(r + 1, 7), s)
    row_peer = [(b, lax.rem(r + d, 8), s) for d in range(1, 8)]
    cross_peer = [(b, lax.rem(r + d, 8), 1 - s) for d in range(1, 8)]
    z = b // 2
    beside = (b + 1 - 2 * (b % 2), r, s)
    above_z = (jnp.minimum(b + 2, 6 + b % 2), r, s)
    below_z = (jnp.maximum(b - 2, b % 2), r, s)

    barrier = pltpu.get_barrier_semaphore()
    for device in [sib, beside] + row_peer + cross_peer:
        pl.semaphore_signal(barrier, inc=1, device_id=device, device_id_type=MESH)

    @pl.when(z < 3)
    def _():
        pl.semaphore_signal(barrier, inc=1, device_id=above_z, device_id_type=MESH)

    @pl.when(z > 0)
    def _():
        pl.semaphore_signal(barrier, inc=1, device_id=below_z, device_id_type=MESH)

    def local(src, dst, i):
        return pltpu.make_async_copy(src, dst, lsem.at[i])

    def remote(src, dst, send, recv, device):
        return pltpu.make_async_remote_copy(
            src_ref=src, dst_ref=dst, send_sem=send, recv_sem=recv, device_id=device, device_id_type=MESH
        )

    loads = {
        "f": local(f, fv, 0),
        "dw": local(dwk, dwv, 1),
        "rid": local(rid, rids.at[r], 2),
        "key": local(key.at[pl.ds(16 * s, 16)], kall.at[s, b * 8 + r], 3),
        "own": local(own, ownv, 4),
        "par": local(par, parv, 5),
        "w1": local(w1, w1v, 6),
        "w2": local(w2, w2v, 7),
        "pe": local(pe, pev, 8),
        "pk": local(pk, pkv, 9),
        "gain": local(gain, gv, 10),
        "scale": local(scale, sv, 11),
    }
    for name in ("dw", "f", "gain", "scale", "rid", "key", "own", "par", "w1", "w2", "pe", "pk"):
        loads[name].start()

    pl.semaphore_wait(barrier, 17 + z * (3 - z) // 2)


    def halo_up(i, h):
        lanes = pl.ds(768 * h, 768)
        return remote(
            f.at[2 * s + i, pl.ds(0, 3), :, lanes], halo.at[i, 1, :, :, lanes],
            hs.at[i, 0, h], hr.at[i, 1, h], up,
        )

    def halo_down(i, h):
        lanes = pl.ds(768 * h, 768)
        return remote(
            f.at[2 * s + i, pl.ds(1, 3), :, lanes], halo.at[i, 0, :, :, lanes],
            hs.at[i, 1, h], hr.at[i, 0, h], down,
        )

    def start_halo(i, h):
        @pl.when(r > 0)
        def _():
            halo_up(i, h).start()

        @pl.when(r < 7)
        def _():
            halo_down(i, h).start()

    def halo_sent(i, h):
        @pl.when(r > 0)
        def _():
            halo_up(i, h).wait_send()

        @pl.when(r < 7)
        def _():
            halo_down(i, h).wait_send()

    start_halo(0, 0)
    rid_copies = [
        remote(rid, rids.at[r], rs1.at[d], rr1.at[d], row_peer[d]) for d in range(7)
    ]
    key_rows = [
        remote(key.at[pl.ds(16 * s, 16)], kall.at[s, b * 8 + r], ks1.at[d], kr1.at[d], row_peer[d])
        for d in range(7)
    ]
    for copy in key_rows:
        copy.start()

    eight = kall.at[s, pl.ds(b * 8, 8)]
    key_beside = remote(eight, eight, ks2.at[0], kr2.at[0], beside)

    def key_up(k):
        plane = kall.at[s, pl.ds(jnp.maximum(z - k, 0) * 16, 16)]
        return remote(plane, plane, kzs.at[0, k], kzr.at[0, k], above_z)

    def key_down(k):
        plane = kall.at[s, pl.ds(jnp.minimum(z + k, 3) * 16, 16)]
        return remote(plane, plane, kzs.at[1, k], kzr.at[1, k], below_z)

    def start_keys(k):
        @pl.when((z < 3) & (z >= k))
        def _():
            key_up(k).start()

        @pl.when((z > 0) & (z + k <= 3))
        def _():
            key_down(k).start()

    def wait_keys(k):
        @pl.when((z < 3) & (z >= k))
        def _():
            key_up(k).wait_send()

        @pl.when((z > 0) & (z + k <= 3))
        def _():
            key_down(k).wait_send()

        @pl.when(z >= k + 1)
        def _():
            key_up(k).wait_recv()

        @pl.when(z + k + 1 <= 3)
        def _():
            key_down(k).wait_recv()

    for i in range(2):
        @pl.when(r == 0)
        def _():
            halo[i, 0] = jnp.zeros_like(halo[i, 0])

        @pl.when(r == 7)
        def _():
            halo[i, 1] = jnp.zeros_like(halo[i, 1])

    loads["dw"].wait()
    for dy in range(7):
        dwf[dy, 0:7, :] = dwv[dy].astype(F32)
    loads["f"].wait()

    col32 = lax.broadcasted_iota(jnp.int32, (32, 128), 0)

    def conv_rows(i, lanes, rows, get, first):
        for y in range(4):
            sums = [None] * 7
            for yi in rows:
                dy = yi - y + 3
                if dy < 0 or dy > 6:
                    continue
                x = get(yi)
                for dx in range(7):
                    term = x * dwf[dy, dx : dx + 1, lanes]
                    sums[dx] = term if sums[dx] is None else sums[dx] + term
            total = sums[3]
            for dx in (0, 1, 2, 4, 5, 6):
                total = total + shifted(sums[dx], 3 - dx, col32)
            if first:
                taps[i, y, :, lanes] = total
            else:
                taps[i, y, :, lanes] = taps[i, y, :, lanes] + total

    def own_part(n, _):
        i = n // 12
        lanes = pl.ds(pl.multiple_of((n % 12) * 128, 128), 128)
        xs = [fv[2 * s + i, y, :, lanes].astype(F32) for y in range(4)]
        conv_rows(i, lanes, range(4), lambda yi: xs[yi], True)
        return 0

    lax.fori_loop(0, 12, own_part, 0)
    start_halo(0, 1)
    lax.fori_loop(12, 24, own_part, 0)

    def halo_part(i, part):
        def step(n, _):
            lanes = pl.ds(pl.multiple_of(n * 128, 128), 128)
            xs = {}
            for k in range(3):
                xs[k - 3] = halo[i, 0, k, :, lanes].astype(F32)
                xs[4 + k] = halo[i, 1, k, :, lanes].astype(F32)
            conv_rows(i, lanes, (-3, -2, -1, 4, 5, 6), lambda yi: xs[yi], False)
            return 0

        lax.fori_loop(6 * part, 6 * part + 6, step, 0)

    def layer_norm(i):
        def step(y, _):
            t = taps[i, y]
            mean = jnp.sum(t, axis=-1, keepdims=True) * (1.0 / 1536)
            t = t - mean
            spread = jnp.sum(t * t, axis=-1, keepdims=True) * (1.0 / 1536)
            out = t * lax.rsqrt(spread + LN_EPS) * gv[...].astype(F32).reshape(1, 1536)
            nrm[i, s, pl.ds(pl.multiple_of(y * 32, 32), 32), :] = out.astype(BF16)
            return 0

        for part in range(2):
            lax.fori_loop(2 * part, 2 * part + 2, step, 0)
            norm_copy(i, part).start()

    def norm_copy(i, part):
        rows = nrm.at[i, s, pl.ds(64 * part, 64)]
        return remote(rows, rows, ns.at[i, part], nr.at[i, part], sib)

    def branch_copy(i, half):
        part = pl.ds(3 * half, 3)
        return remote(bsend.at[i, part], brecv.at[i, part], bs.at[i, half], br.at[i, half], sib)

    def wait_halo(i, h):
        @pl.when(r > 0)
        def _():
            halo_down(i, h).wait_recv()

        @pl.when(r < 7)
        def _():
            halo_up(i, h).wait_recv()

    def tile(n):
        return slice(256 * n, 256 * n + 256)

    def mlp(i):
        x = nrm[i].reshape(256, 1536)
        for n in range(6):
            inner[:, tile(n)] = gelu(dot(x, w1v[:, tile(n)])).astype(BF16)
        for half in range(2):
            for n in range(3 * half, 3 * half + 3):
                h = dot(inner[...], w2v[:, tile(n)])
                bpart[n] = h
                bsend[i, n] = h.astype(BF16)
            branch_copy(i, half).start()

    col192 = lax.broadcasted_iota(jnp.int32, (192, 256), 0) % 32

    def merge(i):
        def merge_tile(n, _):
            lanes = pl.ds(pl.multiple_of(n * 256, 256), 256)
            sc = sv[lanes].astype(F32).reshape(1, 256)
            for h in range(2):
                rows = slice(128 * h, 128 * h + 128)
                base = fv[2 * h + i, :, :, lanes].reshape(128, 256).astype(F32)
                total = bpart[n, rows, :] + brecv[i, n, rows, :].astype(F32)
                bo[rows, lanes] = (base + sc * total).astype(BF16)
            return 0

        for half in range(2):
            branch_copy(i, half).wait()
            lax.fori_loop(3 * half, 3 * half + 3, merge_tile, 0)

    def expand(i):
        for n in range(4):
            hid[:, tile(n)] = jnp.maximum(dot(bo[...], pev[:, tile(n)]), 0.0).astype(BF16)

    def project(i):
        acc[...] = jnp.zeros_like(acc)
        for n in range(9):
            dy, dx = divmod(n, 3)
            h = dot(hid[...], pkv[n])
            rows = slice((2 - dy) * 32, (2 - dy) * 32 + 128)
            for k in range(2):
                acc[k, dx, rows, :] = acc[k, dx, rows, :] + h[128 * k : 128 * k + 128]

        out = None
        for k in range(2):
            total = shifted(acc[k, 0], 1, col192) + acc[k, 1] + shifted(acc[k, 2], -1, col192)
            total = jnp.concatenate([total, jnp.zeros((64, 256), F32)], axis=0)
            for part in split3(total):
                term = dot(spot[2 * k + i], part)
                out = term if out is None else out + term
        if i == 0:
            ordered[...] = out.reshape(8, 32, 256)
        else:
            ordered[...] = ordered[...] + out.reshape(8, 32, 256)

    wait_halo(0, 0)
    halo_part(0, 0)
    for copy in key_rows:
        copy.wait()
    loads["key"].wait()
    key_beside.start()
    halo_sent(0, 0)
    halo_sent(0, 1)
    for copy in rid_copies:
        copy.start()
    start_halo(1, 0)
    loads["gain"].wait()
    loads["scale"].wait()
    wait_halo(0, 1)
    halo_part(0, 1)
    start_halo(1, 1)
    layer_norm(0)
    loads["w1"].wait()
    loads["w2"].wait()

    for part in range(2):
        norm_copy(0, part).wait()
    key_beside.wait()
    start_keys(0)
    mlp(0)

    for copy in rid_copies:
        copy.wait()
    for name in ("rid", "own", "par"):
        loads[name].wait()
    place = lax.broadcasted_iota(jnp.int32, (256, REG), 0)
    reg = lax.broadcasted_iota(jnp.int32, (REG, 256), 0)
    for img in range(4):
        above = jnp.where(r > 0, rids[jnp.maximum(r - 1, 0), img, 3:4, :], -1)
        below = jnp.where(r < 7, rids[jnp.minimum(r + 1, 7), img, 0:1, :], -1)
        rest = jnp.full((1, 64), -1, jnp.int32)
        ids = jnp.concatenate(
            [above] + [rids[r, img, y : y + 1, :] for y in range(4)] + [below, rest], axis=1
        )
        onehot = jnp.where(reg == ids, 1.0, 0.0).astype(BF16)
        perm = jnp.where(place == ownv[:, REG * img : REG * img + REG], 1.0, 0.0).astype(BF16)
        spot[img] = dot(perm, onehot).astype(BF16)

    wait_halo(1, 0)
    halo_part(1, 0)
    wait_halo(1, 1)
    halo_part(1, 1)
    layer_norm(1)
    wait_keys(0)
    start_keys(1)
    halo_sent(1, 0)
    halo_sent(1, 1)
    loads["pe"].wait()
    loads["pk"].wait()
    merge(0)
    expand(0)
    for part in range(2):
        norm_copy(1, part).wait()
    mlp(1)
    project(0)
    wait_keys(1)
    start_keys(2)
    merge(1)
    expand(1)
    project(1)

    ordered16[...] = ordered[...].astype(BF16)
    pool_copies = []
    for d in (2, 6, 3, 5, 1, 7, 4):
        block = ordered16.at[lax.rem(r + d, 8)]
        pool_copies.append(remote(block, gathered.at[0, d], ps.at[0, d], pr.at[0, d], row_peer[d - 1]))
        pool_copies.append(remote(block, gathered.at[1, d], ps.at[1, d], pr.at[1, d], cross_peer[d - 1]))
    pool_copies.append(remote(ordered16.at[r], gathered.at[1, 0], ps.at[1, 0], pr.at[1, 0], sib))
    for copy in pool_copies:
        copy.start()

    key_sib = remote(kall.at[s], kall.at[s], ks3.at[0], kr3.at[0], sib)
    wait_keys(2)
    key_sib.start()
    key_sib.wait()

    ones = jnp.ones((8, 256), BF16)

    def key_norms(n, _):
        k = kall[n // 4, pl.ds(n % 4 * 16, 16)].reshape(256, 256).astype(F32)
        sq = k * k
        top = sq.astype(BF16)
        bottom = (sq - top.astype(F32)).astype(BF16)
        total = dot_t(ones, top) + dot_t(ones, bottom)
        knorm[:, pl.ds(pl.multiple_of(n * 256, 256), 256)] = lax.rsqrt(total + NORM_EPS) * 10.0
        return 0

    lax.fori_loop(0, 8, key_norms, 0)

    slot = lax.broadcasted_iota(jnp.int32, (1, 256), 1)
    partner = jnp.concatenate([parv[k : k + 1, :] for k in range(4)], axis=1)
    target = slot // REG * REG + b * 256 + partner
    positive = (target // 16 % 2 * 1024 + target // 32 * 16 + target % 16).astype(F32)
    used = jnp.zeros((1, 256), F32)
    for k in range(4):
        ids = jnp.max(rids[:, k].astype(F32), axis=0)
        most = jnp.max(jnp.max(ids, axis=1, keepdims=True), axis=0, keepdims=True)
        here = (slot // REG == k) & ((slot % REG).astype(F32) <= most)
        used = jnp.where(here, 1.0, used)
    mine = (lax.broadcasted_iota(jnp.int32, (32, 256), 0) + 32 * r) == ownv[...]
    pos = jnp.sum(jnp.where(mine, positive, 0.0), axis=1, keepdims=True)
    ok = jnp.sum(jnp.where(mine, used, 0.0), axis=1, keepdims=True)

    for copy in pool_copies:
        copy.wait()
    same = ordered16[r].astype(F32)
    cross = gathered[1, 0].astype(F32)
    for d in range(1, 8):
        same = same + gathered[0, d].astype(F32)
        cross = cross + gathered[1, d].astype(F32)
    total = same + cross
    probe = total * lax.rsqrt(jnp.sum(total * total, axis=1, keepdims=True) + NORM_EPS)
    emb_o[...] = probe
    hi, mid, lo = split3(probe)
    keys = kall[...].reshape(2048, 256)
    parts = dot_t(jnp.concatenate([hi, mid, lo], axis=0), keys)
    logits = (parts[0:32] + parts[32:64] + parts[64:96]) * knorm[0:1, :]
    sums = jnp.log(jnp.sum(jnp.exp(logits), axis=1, keepdims=True))
    index = lax.broadcasted_iota(jnp.int32, (32, 2048), 1).astype(F32)
    pos_logit = jnp.sum(jnp.where(index == pos, logits, 0.0), axis=1, keepdims=True)
    loss = jnp.where(ok > 0.5, sums - pos_logit, 0.0)
    eye = lax.broadcasted_iota(jnp.int32, (32, 32), 0) == lax.broadcasted_iota(jnp.int32, (32, 32), 1)
    loss_o[...] = jnp.sum(jnp.where(eye, loss, 0.0), axis=0, keepdims=True)


def finish(emb, loss, emb_o, loss_o):
    emb_o[...] = emb[...]
    loss_o[...] = loss[...]


def body(*args):
    dma = pltpu.SemaphoreType.DMA
    vmem = pltpu.VMEM
    scratch = [
        vmem((4, 4, 32, 1536), BF16),
        vmem((2, 2, 3, 32, 1536), BF16),
        vmem((7, 7, 1536), BF16),
        vmem((7, 8, 1536), F32),
        vmem((1536, 1536), BF16),
        vmem((1536, 1536), BF16),
        vmem((1536, 1024), BF16),
        vmem((9, 1024, 256), BF16),
        vmem((1536,), BF16),
        vmem((1536,), BF16),
        vmem((1, 256), jnp.int32),
        vmem((4, 64), jnp.int32),
        vmem((2, 4, 32, 1536), F32),
        vmem((2, 2, 128, 1536), BF16),
        vmem((256, 1536), BF16),
        vmem((6, 256, 256), F32),
        vmem((2, 6, 256, 256), BF16),
        vmem((2, 6, 256, 256), BF16),
        vmem((256, 1536), BF16),
        vmem((256, 1024), BF16),
        vmem((2, 3, 192, 256), F32),
        vmem((4, 256, 256), BF16),
        vmem((8, 32, 256), F32),
        vmem((8, 32, 256), BF16),
        vmem((2, 8, 32, 256), BF16),
        vmem((8, 4, 4, 32), jnp.int32),
        vmem((2, 64, 16, 256), BF16),
        vmem((8, 2048), F32),
        dma((12,)),
        dma((2, 2, 2)), dma((2, 2, 2)),
        dma((2, 2)), dma((2, 2)),
        dma((2, 2)), dma((2, 2)),
        dma((8,)), dma((8,)),
        dma((8,)), dma((8,)),
        dma((1,)), dma((1,)),
        dma((2, 3)), dma((2, 3)),
        dma((1,)), dma((1,)),
        dma((2, 8)), dma((2, 8)),
    ]
    emb, loss = pl.pallas_call(
        kernel,
        out_shape=(
            jax.ShapeDtypeStruct((32, 256), F32),
            jax.ShapeDtypeStruct((1, 32), F32),
        ),
        in_specs=[pl.BlockSpec(memory_space=pl.ANY)] * 12,
        out_specs=(pl.BlockSpec(memory_space=pltpu.VMEM), pl.BlockSpec(memory_space=pltpu.VMEM)),
        scratch_shapes=scratch,
        compiler_params=pltpu.CompilerParams(
            collective_id=0, has_side_effects=True, vmem_limit_bytes=60 * 1024 * 1024
        ),
        name="region_loss",
    )(*args)
    emb, loss = pl.pallas_call(
        finish,
        out_shape=(
            jax.ShapeDtypeStruct((32, 256), F32),
            jax.ShapeDtypeStruct((1, 32), F32),
        ),
        in_specs=[pl.BlockSpec(memory_space=pltpu.VMEM)] * 2,
        out_specs=(pl.BlockSpec(memory_space=pltpu.VMEM), pl.BlockSpec(memory_space=pltpu.VMEM)),
        name="finish",
    )(emb, loss)
    return emb, loss.reshape(32)


def solution(mesh):
    in_specs = (
        P("batch", "rows", None, None),
        P(),
        P(),
        P(None, "section"),
        P("section", None),
        P(),
        P(None, "section"),
        P(None, "section", None),
        P("batch", "rows", None),
        P("batch", None),
        P("batch", None),
        P(("batch", "rows"), None),
    )
    out_specs = (P(("batch", "rows"), None), P(("batch", "rows")))
    return jax.shard_map(body, mesh=mesh, in_specs=in_specs, out_specs=out_specs, check_vma=False)
```

```python
import jax
import jax.numpy as jnp
from jax import lax
from jax.experimental import pallas as pl
from jax.experimental.pallas import tpu as pltpu
from jax.sharding import PartitionSpec as P

MESH = pl.DeviceIdType.MESH
REG = 64
LN_EPS = 1e-06
NORM_EPS = 1e-06
F32 = jnp.float32
BF16 = jnp.bfloat16


def split3(x):
    hi = x.astype(BF16)
    rest = x - hi.astype(F32)
    mid = rest.astype(BF16)
    lo = (rest - mid.astype(F32)).astype(BF16)
    return hi, mid, lo


def dot(a, b):
    return jnp.dot(a, b, preferred_element_type=F32)


def dot_t(a, b):
    return lax.dot_general(a, b, (((1,), (1,)), ((), ())), preferred_element_type=F32)


def gelu(x):
    return 0.5 * x * (1.0 + lax.erf(x * 0.7071067811865476))


def shifted(x, by, col):
    if by == 0:
        return x
    n = x.shape[0]
    moved = pltpu.roll(x, by % n, 0)
    keep = (col >= by) if by > 0 else (col < 32 + by)
    return jnp.where(keep, moved, 0.0)


def kernel(
    f, dwk, gain, w1, w2, scale, pe, pk, rid, own, par, key,
    emb_o, loss_o,
    fv, halo, dwv, dwf, w1v, w2v, pev, pkv, gv, sv, ownv, parv,
    taps, nrm, inner, bpart, bsend, brecv, bo, hid, acc, spot, ordered, ordered16, gathered,
    rids, kall, knorm,
    lsem, hs, hr, ns, nr, bs, br, rs1, rr1, ks1, kr1, ks2, kr2, kzs, kzr, ks3, kr3, ps, pr,
):
    b = lax.axis_index("batch")
    r = lax.axis_index("rows")
    s = lax.axis_index("section")
    sib = (b, r, 1 - s)
    up = (b, jnp.maximum(r - 1, 0), s)
    down = (b, jnp.minimum(r + 1, 7), s)
    row_peer = [(b, lax.rem(r + d, 8), s) for d in range(1, 8)]
    cross_peer = [(b, lax.rem(r + d, 8), 1 - s) for d in range(1, 8)]
    z = b // 2
    beside = (b + 1 - 2 * (b % 2), r, s)
    above_z = (jnp.minimum(b + 2, 6 + b % 2), r, s)
    below_z = (jnp.maximum(b - 2, b % 2), r, s)

    barrier = pltpu.get_barrier_semaphore()
    for device in [sib, beside] + row_peer + cross_peer:
        pl.semaphore_signal(barrier, inc=1, device_id=device, device_id_type=MESH)

    @pl.when(z < 3)
    def _():
        pl.semaphore_signal(barrier, inc=1, device_id=above_z, device_id_type=MESH)

    @pl.when(z > 0)
    def _():
        pl.semaphore_signal(barrier, inc=1, device_id=below_z, device_id_type=MESH)

    def local(src, dst, i):
        return pltpu.make_async_copy(src, dst, lsem.at[i])

    def remote(src, dst, send, recv, device):
        return pltpu.make_async_remote_copy(
            src_ref=src, dst_ref=dst, send_sem=send, recv_sem=recv, device_id=device, device_id_type=MESH
        )

    loads = {
        "f": local(f, fv, 0),
        "dw": local(dwk, dwv, 1),
        "rid": local(rid, rids.at[r], 2),
        "key": local(key.at[pl.ds(16 * s, 16)], kall.at[s, b * 8 + r], 3),
        "own": local(own, ownv, 4),
        "par": local(par, parv, 5),
        "w1": local(w1, w1v, 6),
        "w2": local(w2, w2v, 7),
        "pe": local(pe, pev, 8),
        "pk": local(pk, pkv, 9),
        "gain": local(gain, gv, 10),
        "scale": local(scale, sv, 11),
    }
    for name in ("dw", "f", "gain", "scale", "rid", "key", "own", "par", "w1", "w2", "pe", "pk"):
        loads[name].start()

    pl.semaphore_wait(barrier, 17 + z * (3 - z) // 2)


    def halo_up(i, h):
        lanes = pl.ds(768 * h, 768)
        return remote(
            f.at[2 * s + i, pl.ds(0, 3), :, lanes], halo.at[i, 1, :, :, lanes],
            hs.at[i, 0, h], hr.at[i, 1, h], up,
        )

    def halo_down(i, h):
        lanes = pl.ds(768 * h, 768)
        return remote(
            f.at[2 * s + i, pl.ds(1, 3), :, lanes], halo.at[i, 0, :, :, lanes],
            hs.at[i, 1, h], hr.at[i, 0, h], down,
        )

    def start_halo(i, h):
        @pl.when(r > 0)
        def _():
            halo_up(i, h).start()

        @pl.when(r < 7)
        def _():
            halo_down(i, h).start()

    def halo_sent(i, h):
        @pl.when(r > 0)
        def _():
            halo_up(i, h).wait_send()

        @pl.when(r < 7)
        def _():
            halo_down(i, h).wait_send()

    start_halo(0, 0)
    rid_copies = [
        remote(rid, rids.at[r], rs1.at[d], rr1.at[d], row_peer[d]) for d in range(7)
    ]
    key_rows = [
        remote(key.at[pl.ds(16 * s, 16)], kall.at[s, b * 8 + r], ks1.at[d], kr1.at[d], row_peer[d])
        for d in range(7)
    ]
    for copy in key_rows:
        copy.start()

    eight = kall.at[s, pl.ds(b * 8, 8)]
    key_beside = remote(eight, eight, ks2.at[0], kr2.at[0], beside)

    def key_up(k):
        plane = kall.at[s, pl.ds(jnp.maximum(z - k, 0) * 16, 16)]
        return remote(plane, plane, kzs.at[0, k], kzr.at[0, k], above_z)

    def key_down(k):
        plane = kall.at[s, pl.ds(jnp.minimum(z + k, 3) * 16, 16)]
        return remote(plane, plane, kzs.at[1, k], kzr.at[1, k], below_z)

    def start_keys(k):
        @pl.when((z < 3) & (z >= k))
        def _():
            key_up(k).start()

        @pl.when((z > 0) & (z + k <= 3))
        def _():
            key_down(k).start()

    def wait_keys(k):
        @pl.when((z < 3) & (z >= k))
        def _():
            key_up(k).wait_send()

        @pl.when((z > 0) & (z + k <= 3))
        def _():
            key_down(k).wait_send()

        @pl.when(z >= k + 1)
        def _():
            key_up(k).wait_recv()

        @pl.when(z + k + 1 <= 3)
        def _():
            key_down(k).wait_recv()

    for i in range(2):
        @pl.when(r == 0)
        def _():
            halo[i, 0] = jnp.zeros_like(halo[i, 0])

        @pl.when(r == 7)
        def _():
            halo[i, 1] = jnp.zeros_like(halo[i, 1])

    loads["dw"].wait()
    for dy in range(7):
        dwf[dy, 0:7, :] = dwv[dy].astype(F32)
    loads["f"].wait()

    col32 = lax.broadcasted_iota(jnp.int32, (32, 128), 0)

    def conv_rows(i, lanes, rows, get, first):
        for y in range(4):
            sums = [None] * 7
            for yi in rows:
                dy = yi - y + 3
                if dy < 0 or dy > 6:
                    continue
                x = get(yi)
                for dx in range(7):
                    term = x * dwf[dy, dx : dx + 1, lanes]
                    sums[dx] = term if sums[dx] is None else sums[dx] + term
            total = sums[3]
            for dx in (0, 1, 2, 4, 5, 6):
                total = total + shifted(sums[dx], 3 - dx, col32)
            if first:
                taps[i, y, :, lanes] = total
            else:
                taps[i, y, :, lanes] = taps[i, y, :, lanes] + total

    def own_part(n, _):
        i = n // 12
        lanes = pl.ds(pl.multiple_of((n % 12) * 128, 128), 128)
        xs = [fv[2 * s + i, y, :, lanes].astype(F32) for y in range(4)]
        conv_rows(i, lanes, range(4), lambda yi: xs[yi], True)
        return 0

    lax.fori_loop(0, 12, own_part, 0)
    start_halo(0, 1)
    lax.fori_loop(12, 24, own_part, 0)

    def halo_part(i, part):
        def step(n, _):
            lanes = pl.ds(pl.multiple_of(n * 128, 128), 128)
            xs = {}
            for k in range(3):
                xs[k - 3] = halo[i, 0, k, :, lanes].astype(F32)
                xs[4 + k] = halo[i, 1, k, :, lanes].astype(F32)
            conv_rows(i, lanes, (-3, -2, -1, 4, 5, 6), lambda yi: xs[yi], False)
            return 0

        lax.fori_loop(6 * part, 6 * part + 6, step, 0)

    def layer_norm(i):
        def step(y, _):
            t = taps[i, y]
            mean = jnp.sum(t, axis=-1, keepdims=True) * (1.0 / 1536)
            t = t - mean
            spread = jnp.sum(t * t, axis=-1, keepdims=True) * (1.0 / 1536)
            out = t * lax.rsqrt(spread + LN_EPS) * gv[...].astype(F32).reshape(1, 1536)
            nrm[i, s, pl.ds(pl.multiple_of(y * 32, 32), 32), :] = out.astype(BF16)
            return 0

        for part in range(2):
            lax.fori_loop(2 * part, 2 * part + 2, step, 0)
            norm_copy(i, part).start()

    def norm_copy(i, part):
        rows = nrm.at[i, s, pl.ds(64 * part, 64)]
        return remote(rows, rows, ns.at[i, part], nr.at[i, part], sib)

    def branch_copy(i, half):
        part = pl.ds(3 * half, 3)
        return remote(bsend.at[i, part], brecv.at[i, part], bs.at[i, half], br.at[i, half], sib)

    def wait_halo(i, h):
        @pl.when(r > 0)
        def _():
            halo_down(i, h).wait_recv()

        @pl.when(r < 7)
        def _():
            halo_up(i, h).wait_recv()

    def tile(n):
        return slice(256 * n, 256 * n + 256)

    def mlp(i):
        x = nrm[i].reshape(256, 1536)
        for n in range(6):
            inner[:, tile(n)] = gelu(dot(x, w1v[:, tile(n)])).astype(BF16)
        for half in range(2):
            for n in range(3 * half, 3 * half + 3):
                h = dot(inner[...], w2v[:, tile(n)])
                bpart[n] = h
                bsend[i, n] = h.astype(BF16)
            branch_copy(i, half).start()

    col192 = lax.broadcasted_iota(jnp.int32, (192, 256), 0) % 32

    def merge(i):
        def merge_tile(n, _):
            lanes = pl.ds(pl.multiple_of(n * 256, 256), 256)
            sc = sv[lanes].astype(F32).reshape(1, 256)
            for h in range(2):
                rows = slice(128 * h, 128 * h + 128)
                base = fv[2 * h + i, :, :, lanes].reshape(128, 256).astype(F32)
                total = bpart[n, rows, :] + brecv[i, n, rows, :].astype(F32)
                bo[rows, lanes] = (base + sc * total).astype(BF16)
            return 0

        for half in range(2):
            branch_copy(i, half).wait()
            lax.fori_loop(3 * half, 3 * half + 3, merge_tile, 0)

    def expand(i):
        for n in range(4):
            hid[:, tile(n)] = jnp.maximum(dot(bo[...], pev[:, tile(n)]), 0.0).astype(BF16)

    def project(i):
        acc[...] = jnp.zeros_like(acc)
        for n in range(9):
            dy, dx = divmod(n, 3)
            h = dot(hid[...], pkv[n])
            rows = slice((2 - dy) * 32, (2 - dy) * 32 + 128)
            for k in range(2):
                acc[k, dx, rows, :] = acc[k, dx, rows, :] + h[128 * k : 128 * k + 128]

        out = None
        for k in range(2):
            total = shifted(acc[k, 0], 1, col192) + acc[k, 1] + shifted(acc[k, 2], -1, col192)
            total = jnp.concatenate([total, jnp.zeros((64, 256), F32)], axis=0)
            for part in split3(total):
                term = dot(spot[2 * k + i], part)
                out = term if out is None else out + term
        if i == 0:
            ordered[...] = out.reshape(8, 32, 256)
        else:
            ordered[...] = ordered[...] + out.reshape(8, 32, 256)

    wait_halo(0, 0)
    halo_part(0, 0)
    for copy in key_rows:
        copy.wait()
    loads["key"].wait()
    key_beside.start()
    halo_sent(0, 0)
    halo_sent(0, 1)
    for copy in rid_copies:
        copy.start()
    start_halo(1, 0)
    loads["gain"].wait()
    loads["scale"].wait()
    wait_halo(0, 1)
    halo_part(0, 1)
    start_halo(1, 1)
    layer_norm(0)
    loads["w1"].wait()
    loads["w2"].wait()

    for part in range(2):
        norm_copy(0, part).wait()
    key_beside.wait()
    start_keys(0)
    mlp(0)

    for copy in rid_copies:
        copy.wait()
    for name in ("rid", "own", "par"):
        loads[name].wait()
    place = lax.broadcasted_iota(jnp.int32, (256, REG), 0)
    reg = lax.broadcasted_iota(jnp.int32, (REG, 256), 0)
    for img in range(4):
        above = jnp.where(r > 0, rids[jnp.maximum(r - 1, 0), img, 3:4, :], -1)
        below = jnp.where(r < 7, rids[jnp.minimum(r + 1, 7), img, 0:1, :], -1)
        rest = jnp.full((1, 64), -1, jnp.int32)
        ids = jnp.concatenate(
            [above] + [rids[r, img, y : y + 1, :] for y in range(4)] + [below, rest], axis=1
        )
        onehot = jnp.where(reg == ids, 1.0, 0.0).astype(BF16)
        perm = jnp.where(place == ownv[:, REG * img : REG * img + REG], 1.0, 0.0).astype(BF16)
        spot[img] = dot(perm, onehot).astype(BF16)

    wait_halo(1, 0)
    halo_part(1, 0)
    wait_halo(1, 1)
    halo_part(1, 1)
    layer_norm(1)
    wait_keys(0)
    start_keys(1)
    halo_sent(1, 0)
    halo_sent(1, 1)
    loads["pe"].wait()
    loads["pk"].wait()
    merge(0)
    expand(0)
    for part in range(2):
        norm_copy(1, part).wait()
    mlp(1)
    project(0)
    wait_keys(1)
    start_keys(2)
    merge(1)
    expand(1)
    project(1)

    ordered16[...] = ordered[...].astype(BF16)
    pool_copies = []
    for d in (2, 6, 3, 5, 1, 7, 4):
        block = ordered16.at[lax.rem(r + d, 8)]
        pool_copies.append(remote(block, gathered.at[0, d], ps.at[0, d], pr.at[0, d], row_peer[d - 1]))
        pool_copies.append(remote(block, gathered.at[1, d], ps.at[1, d], pr.at[1, d], cross_peer[d - 1]))
    pool_copies.append(remote(ordered16.at[r], gathered.at[1, 0], ps.at[1, 0], pr.at[1, 0], sib))
    for copy in pool_copies:
        copy.start()

    key_sib = remote(kall.at[s], kall.at[s], ks3.at[0], kr3.at[0], sib)
    wait_keys(2)
    key_sib.start()

    ones = jnp.ones((8, 256), BF16)

    def key_norms(n, _):
        k = kall[n // 4, pl.ds(n % 4 * 16, 16)].reshape(256, 256).astype(F32)
        sq = k * k
        top = sq.astype(BF16)
        bottom = (sq - top.astype(F32)).astype(BF16)
        total = dot_t(ones, top) + dot_t(ones, bottom)
        knorm[:, pl.ds(pl.multiple_of(n * 256, 256), 256)] = lax.rsqrt(total + NORM_EPS) * 10.0
        return 0

    lax.fori_loop(4 * s, 4 * s + 4, key_norms, 0)
    key_sib.wait()
    lax.fori_loop(4 - 4 * s, 8 - 4 * s, key_norms, 0)

    slot = lax.broadcasted_iota(jnp.int32, (1, 256), 1)
    partner = jnp.concatenate([parv[k : k + 1, :] for k in range(4)], axis=1)
    target = slot // REG * REG + b * 256 + partner
    positive = (target // 16 % 2 * 1024 + target // 32 * 16 + target % 16).astype(F32)
    used = jnp.zeros((1, 256), F32)
    for k in range(4):
        ids = jnp.max(rids[:, k].astype(F32), axis=0)
        most = jnp.max(jnp.max(ids, axis=1, keepdims=True), axis=0, keepdims=True)
        here = (slot // REG == k) & ((slot % REG).astype(F32) <= most)
        used = jnp.where(here, 1.0, used)
    mine = (lax.broadcasted_iota(jnp.int32, (32, 256), 0) + 32 * r) == ownv[...]
    pos = jnp.sum(jnp.where(mine, positive, 0.0), axis=1, keepdims=True)
    ok = jnp.sum(jnp.where(mine, used, 0.0), axis=1, keepdims=True)

    for copy in pool_copies:
        copy.wait()
    same = ordered16[r].astype(F32)
    cross = gathered[1, 0].astype(F32)
    for d in range(1, 8):
        same = same + gathered[0, d].astype(F32)
        cross = cross + gathered[1, d].astype(F32)
    total = same + cross
    probe = total * lax.rsqrt(jnp.sum(total * total, axis=1, keepdims=True) + NORM_EPS)
    emb_o[...] = probe
    hi, mid, lo = split3(probe)
    keys = kall[...].reshape(2048, 256)
    parts = dot_t(jnp.concatenate([hi, mid, lo], axis=0), keys)
    logits = (parts[0:32] + parts[32:64] + parts[64:96]) * knorm[0:1, :]
    sums = jnp.log(jnp.sum(jnp.exp(logits), axis=1, keepdims=True))
    index = lax.broadcasted_iota(jnp.int32, (32, 2048), 1).astype(F32)
    pos_logit = jnp.sum(jnp.where(index == pos, logits, 0.0), axis=1, keepdims=True)
    loss = jnp.where(ok > 0.5, sums - pos_logit, 0.0)
    eye = lax.broadcasted_iota(jnp.int32, (32, 32), 0) == lax.broadcasted_iota(jnp.int32, (32, 32), 1)
    loss_o[...] = jnp.sum(jnp.where(eye, loss, 0.0), axis=0, keepdims=True)


def finish(emb, loss, emb_o, loss_o):
    emb_o[...] = emb[...]
    loss_o[...] = loss[...]


def body(*args):
    dma = pltpu.SemaphoreType.DMA
    vmem = pltpu.VMEM
    scratch = [
        vmem((4, 4, 32, 1536), BF16),
        vmem((2, 2, 3, 32, 1536), BF16),
        vmem((7, 7, 1536), BF16),
        vmem((7, 8, 1536), F32),
        vmem((1536, 1536), BF16),
        vmem((1536, 1536), BF16),
        vmem((1536, 1024), BF16),
        vmem((9, 1024, 256), BF16),
        vmem((1536,), BF16),
        vmem((1536,), BF16),
        vmem((1, 256), jnp.int32),
        vmem((4, 64), jnp.int32),
        vmem((2, 4, 32, 1536), F32),
        vmem((2, 2, 128, 1536), BF16),
        vmem((256, 1536), BF16),
        vmem((6, 256, 256), F32),
        vmem((2, 6, 256, 256), BF16),
        vmem((2, 6, 256, 256), BF16),
        vmem((256, 1536), BF16),
        vmem((256, 1024), BF16),
        vmem((2, 3, 192, 256), F32),
        vmem((4, 256, 256), BF16),
        vmem((8, 32, 256), F32),
        vmem((8, 32, 256), BF16),
        vmem((2, 8, 32, 256), BF16),
        vmem((8, 4, 4, 32), jnp.int32),
        vmem((2, 64, 16, 256), BF16),
        vmem((8, 2048), F32),
        dma((12,)),
        dma((2, 2, 2)), dma((2, 2, 2)),
        dma((2, 2)), dma((2, 2)),
        dma((2, 2)), dma((2, 2)),
        dma((8,)), dma((8,)),
        dma((8,)), dma((8,)),
        dma((1,)), dma((1,)),
        dma((2, 3)), dma((2, 3)),
        dma((1,)), dma((1,)),
        dma((2, 8)), dma((2, 8)),
    ]
    emb, loss = pl.pallas_call(
        kernel,
        out_shape=(
            jax.ShapeDtypeStruct((32, 256), F32),
            jax.ShapeDtypeStruct((1, 32), F32),
        ),
        in_specs=[pl.BlockSpec(memory_space=pl.ANY)] * 12,
        out_specs=(pl.BlockSpec(memory_space=pltpu.VMEM), pl.BlockSpec(memory_space=pltpu.VMEM)),
        scratch_shapes=scratch,
        compiler_params=pltpu.CompilerParams(
            collective_id=0, has_side_effects=True, vmem_limit_bytes=60 * 1024 * 1024
        ),
        name="region_loss",
    )(*args)
    emb, loss = pl.pallas_call(
        finish,
        out_shape=(
            jax.ShapeDtypeStruct((32, 256), F32),
            jax.ShapeDtypeStruct((1, 32), F32),
        ),
        in_specs=[pl.BlockSpec(memory_space=pltpu.VMEM)] * 2,
        out_specs=(pl.BlockSpec(memory_space=pltpu.VMEM), pl.BlockSpec(memory_space=pltpu.VMEM)),
        name="finish",
    )(emb, loss)
    return emb, loss.reshape(32)


def solution(mesh):
    in_specs = (
        P("batch", "rows", None, None),
        P(),
        P(),
        P(None, "section"),
        P("section", None),
        P(),
        P(None, "section"),
        P(None, "section", None),
        P("batch", "rows", None),
        P("batch", None),
        P("batch", None),
        P(("batch", "rows"), None),
    )
    out_specs = (P(("batch", "rows"), None), P(("batch", "rows")))
    return jax.shard_map(body, mesh=mesh, in_specs=in_specs, out_specs=out_specs, check_vma=False)
```
